32 devices in a mesh: freq: 4 (over y, core), row: 4 (over z), col: 2 (over x).
Axes of the slice: x: 2, y: 2, z: 4, core: 2. Of those that a mesh axis runs over, the one named last changes fastest.
Arguments:
- voltages: bfloat16 [128, 259, 2048], P(('row', 'col', 'freq')), may hold values from -128 to 127, as said below
- tap_table: int32 [4, 2048], replicated, may hold values from -4096 to 4095
Outputs:
- visibility: float32 [1024, 2, 4, 32, 128], P('freq', None, None, 'col', 'row')
The draws below stay inside these ranges and needn't reach their ends.
Inputs may be any that keep to these rules, and one draw needn't show every extreme that they name: `voltages`: whole numbers.
All inputs are finite; a program needn't handle non-finite values.
Results may differ from the reference program's by a relative error of at most 0.0033.
Values may be sent and summed in bfloat16 or wider, within the bound.
No kernel may reach another device: no remote copies, remote signals or barrier semaphores. Data moves between devices by JAX's collectives and lax.ppermute only.
A program may use at most 192 MiB of HBM per device.

```python
import math
import jax
import jax.numpy as jnp
from jax import lax

NFFT = 2048
TAPS = 4
SPEC = 256
CHAN = 1024
INPUTS = 128
FRAMES = 259
N_ROW = 4


def draw_voltages(key, part):
    shape = (INPUTS, FRAMES, NFFT)
    values = jax.random.randint(jax.random.fold_in(key, 10), shape, -128, 128)
    return values.astype(jnp.float32).astype(jnp.bfloat16)


def plant(drawn, rng, low, top_value):
    longest = drawn.shape.index(max(drawn.shape))
    spots = []
    for shift in (0, 1):
        where = [jax.random.randint(jax.random.fold_in(rng, axis), (), 0, length) for axis, length in enumerate(drawn.shape)]
        where[longest] = (where[longest] + shift) % drawn.shape[longest]
        spots.append(tuple(where))
    return drawn.at[spots[0]].set(low).at[spots[1]].set(top_value)


def setup_inputs(seed: int = 0) -> dict:
    key_of = jax.random.split(jax.random.key(seed), 3)
    voltages = draw_voltages(jax.random.fold_in(key_of[2], 71), 0)
    tap_table = plant(jax.random.randint(key_of[1], (TAPS, NFFT), -4096, 4096), jax.random.fold_in(key_of[1], 1), -4096, 4095).astype(jnp.int32)
    return dict(voltages=voltages, tap_table=tap_table)


def filter_block(volt_rows, tap_table):
    weights = tap_table.astype(jnp.float32) / 4096.0
    filtered = weights[0] * volt_rows[:, 0:SPEC, :].astype(jnp.float32)
    for tap_index in range(1, TAPS):
        filtered = filtered + weights[tap_index] * volt_rows[:, tap_index:tap_index + SPEC, :].astype(jnp.float32)
    spectrum = jnp.fft.rfft(filtered, axis=-1)[..., :CHAN] / (64.0 * math.sqrt(NFFT))
    return (jnp.real(spectrum).astype(jnp.bfloat16), jnp.imag(spectrum).astype(jnp.bfloat16))

def correlate_block(pair):
    real_rows = pair[0].astype(jnp.float32)
    imag_rows = pair[1].astype(jnp.float32)
    highest = lax.Precision.HIGHEST
    real_vis = jnp.einsum('cjt,cit->cji', real_rows, real_rows, precision=highest) + jnp.einsum('cjt,cit->cji', imag_rows, imag_rows, precision=highest)
    imag_vis = jnp.einsum('cjt,cit->cji', real_rows, imag_rows, precision=highest) - jnp.einsum('cjt,cit->cji', imag_rows, real_rows, precision=highest)
    return jnp.stack([real_vis, imag_vis], axis=1) / SPEC

def reference(voltages, tap_table):
    blocks = voltages.reshape(INPUTS // 16, 16, FRAMES, NFFT)
    real_part, imag_part = lax.map(lambda volt_rows: filter_block(volt_rows, tap_table), blocks)
    real_part = real_part.reshape(INPUTS, SPEC, CHAN).transpose(2, 0, 1).reshape(CHAN // 8, 8, INPUTS, SPEC)
    imag_part = imag_part.reshape(INPUTS, SPEC, CHAN).transpose(2, 0, 1).reshape(CHAN // 8, 8, INPUTS, SPEC)
    result = lax.map(correlate_block, (real_part, imag_part))
    return result.reshape(CHAN, 2, N_ROW, INPUTS // N_ROW, INPUTS)
```

```python
import functools
import math

import jax
import jax.numpy as jnp
import numpy as np
from jax import lax
from jax.experimental import pallas as pl
from jax.experimental.pallas import tpu as pltpu
from jax.sharding import PartitionSpec as P

OWNERS = ("col", "row")
EVERYONE = ("col", "row", "freq")


def split(value):
    high = value.astype(jnp.bfloat16)
    low = (value - high.astype(jnp.float32)).astype(jnp.bfloat16)
    return high, low


def dft_tables(length, channels, parity, groups):
    half = length // 2
    stride = 2 ** ((channels.bit_length() - 1) // 2)
    sample = np.arange(half)
    coarse = 2.0 * math.pi / length * ((np.arange(0, channels, stride)[:, None] * sample) % length)
    fine = 2.0 * math.pi / length * ((np.arange(parity, stride, 2)[:, None] * sample) % length)
    factor = 1.0 / (64.0 * math.sqrt(length))
    cos_a, sin_a = (jnp.asarray((f(coarse) * factor)[:, None], jnp.float32) for f in (np.cos, np.sin))
    cos_b, sin_b = (jnp.asarray(f(fine)[None], jnp.float32) for f in (np.cos, np.sin))
    real = (cos_a * cos_b - sin_a * sin_b).reshape(groups, -1, half)
    imag = (-(sin_a * cos_b) - cos_a * sin_b).reshape(groups, -1, half)
    return split(jnp.stack([real, imag], axis=1).reshape(groups, -1, half))


def dft_kernel(owners, table_high, table_low, data_high, data_low, out):
    dims = (((1,), (1,)), ((), ()))
    dot = functools.partial(lax.dot_general, dimension_numbers=dims, preferred_element_type=jnp.float32)
    high, low = table_high[0], table_low[0]
    result = dot(high, data_high[...]) + (dot(high, data_low[...]) + dot(low, data_high[...]))
    result = result.astype(jnp.bfloat16)
    count = out.shape[3]
    for part in range(2):
        for owner in range(owners):
            start = (part * owners + owner) * count
            out[owner, 0, part] = result[start : start + count]


def dft(tables, data, groups, owners):
    table_high, table_low = tables
    data_high, data_low = data
    rows, half = table_high.shape[1:]
    width = data_high.shape[0]
    count = rows // 2 // owners
    table_spec = pl.BlockSpec((1, rows, half), lambda g: (g, 0, 0))
    data_spec = pl.BlockSpec((width, half), lambda g: (0, 0))
    return pl.pallas_call(
        functools.partial(dft_kernel, owners),
        grid=(groups,),
        in_specs=[table_spec, table_spec, data_spec, data_spec],
        out_specs=pl.BlockSpec((owners, 1, 2, count, width), lambda g: (0, g, 0, 0, 0)),
        out_shape=jax.ShapeDtypeStruct((owners, groups, 2, count, width), jnp.bfloat16),
        cost_estimate=pl.CostEstimate(
            flops=6 * groups * rows * half * width,
            bytes_accessed=4 * (groups * rows * half + width * half) + 2 * groups * rows * width,
            transcendentals=0,
        ),
    )(table_high, table_low, data_high, data_low)


def shards(voltages, tap_table):
    groups, row_count, col_count = (lax.axis_size(name) for name in ("freq", "row", "col"))
    owners = row_count * col_count
    inputs, frames, length = voltages.shape
    taps = tap_table.shape[0]
    spec_count = frames - taps + 1
    channels, half = length // 2, length // 2
    weights = tap_table.astype(jnp.float32) / 4096.0
    filtered = weights[0] * voltages[:, 0:spec_count, :].astype(jnp.float32)
    for k in range(1, taps):
        filtered = filtered + weights[k] * voltages[:, k : k + spec_count, :].astype(jnp.float32)
    first, second = filtered[..., :half], filtered[..., half:]
    sent = []
    for parity, folded in enumerate((first + second, first - second)):
        data = split(folded.reshape(inputs * spec_count, half))
        sent.append(dft(dft_tables(length, channels, parity, groups), data, groups, owners))
    sent = jnp.stack(sent, axis=4)
    count = sent.shape[3]
    got = lax.all_to_all(
        sent.reshape(owners * groups, 2, 2 * count, inputs * spec_count), EVERYONE, split_axis=0, concat_axis=0, tiled=True
    )
    got = got.reshape(col_count, row_count, groups, 2, 2 * count, inputs, spec_count)
    got = got.transpose(4, 3, 1, 0, 2, 5, 6).reshape(2 * count, 2, -1, spec_count)
    turned = jnp.stack([-got[:, 1], got[:, 0]], axis=1)
    stacked = jnp.concatenate([got, turned], axis=2)
    products = jnp.einsum("cpjt,cpit->cji", stacked, got, preferred_element_type=jnp.float32) / spec_count
    block = groups * inputs
    products = products.astype(jnp.bfloat16).reshape(2 * count, 2, row_count, col_count, block, row_count, col_count * block)
    products = products.transpose(3, 5, 0, 1, 2, 4, 6).reshape(owners, 2 * count, 2, row_count * block, col_count * block)
    back = lax.all_to_all(products, OWNERS, split_axis=0, concat_axis=0, tiled=True)
    back = back.reshape(owners * 2 * count, 2, row_count, block, col_count * block)
    return back.astype(jnp.float32)


def solution(mesh):
    in_specs = (P(("row", "col", "freq"), None, None), P())
    out_specs = P("freq", None, None, "col", "row")
    return jax.shard_map(shards, mesh=mesh, in_specs=in_specs, out_specs=out_specs, check_vma=False)
```

```python
import functools
import math

import jax
import jax.numpy as jnp
import numpy as np
from jax import lax
from jax.experimental import pallas as pl
from jax.experimental.pallas import tpu as pltpu
from jax.sharding import PartitionSpec as P

OWNERS = ("col", "row")
EVERYONE = ("col", "row", "freq")
ROWS_ALIKE = (((1,), (1,)), ((), ()))
WHOLE = pl.BlockSpec(memory_space=pltpu.VMEM)


def split(value):
    high = value.astype(jnp.bfloat16)
    low = (value - high.astype(jnp.float32)).astype(jnp.bfloat16)
    return high, low


def dft_tables(length, channels, parity, groups):
    half = length // 2
    stride = 2 ** ((channels.bit_length() - 1) // 2)
    sample = np.arange(half)
    factor = 1.0 / (64.0 * math.sqrt(length))
    coarse = 2.0 * math.pi / length * ((np.arange(0, channels, stride)[:, None] * sample) % length)
    fine = 2.0 * math.pi / length * ((np.arange(parity, stride, 2)[:, None] * sample) % length)
    coarse = np.stack([np.cos(coarse), np.sin(coarse)], axis=1) * factor
    fine = np.stack([np.cos(fine), np.sin(fine)])
    return jnp.asarray(coarse.reshape(groups, -1, half), jnp.float32), jnp.asarray(fine, jnp.float32)


def dft_kernel(parity, owners, volts, taps, coarse, fine, out, fold, high, low, table_high, table_low):
    frames, inputs, length = volts.shape
    half = length // 2
    tap_count = taps.shape[0]
    spec_count = frames - tap_count + 1
    step, lanes = 8, 128
    rows = step * inputs

    @pl.when(pl.program_id(0) == 0)
    def _():
        for start in range(0, half, lanes):
            pair = (start, start + half)
            weights = [taps[:, pl.ds(at, lanes)].astype(jnp.float32) / 4096.0 for at in pair]

            def filter_rows(index, carry):
                total = None
                for at, weight in zip(pair, weights):
                    block = volts[pl.ds(index * step, step + tap_count - 1), :, pl.ds(at, lanes)].astype(jnp.float32)
                    block = block.reshape(-1, lanes)
                    value = weight[0:1] * block[:rows]
                    for k in range(1, tap_count):
                        value = value + weight[k : k + 1] * block[k * inputs : k * inputs + rows]
                    total = value if total is None else (total - value if parity else total + value)
                fold[pl.ds(pl.multiple_of(index * rows, rows), rows), :] = total
                return carry

            lax.fori_loop(0, spec_count // step, filter_rows, 0)
            for i in range(inputs):
                high_part, low_part = split(fold[pl.ds(i, spec_count, stride=inputs), :])
                high[pl.ds(i * spec_count, spec_count), pl.ds(start, lanes)] = high_part
                low[pl.ds(i * spec_count, spec_count), pl.ds(start, lanes)] = low_part

    fine_count = fine.shape[1]
    group_rows = table_high.shape[0] // 2
    for a in range(group_rows // fine_count):
        cos_a, sin_a = coarse[0, 2 * a : 2 * a + 1], coarse[0, 2 * a + 1 : 2 * a + 2]
        real = cos_a * fine[0] - sin_a * fine[1]
        imag = -(sin_a * fine[0]) - cos_a * fine[1]
        for part, value in enumerate((real, imag)):
            at = pl.ds(part * group_rows + a * fine_count, fine_count)
            table_high[at], table_low[at] = split(value)

    dot = functools.partial(lax.dot_general, dimension_numbers=ROWS_ALIKE, preferred_element_type=jnp.float32)
    result = dot(table_high[...], high[...]) + (dot(table_high[...], low[...]) + dot(table_low[...], high[...]))
    result = result.astype(jnp.bfloat16)
    count = out.shape[3]
    for part in range(2):
        for owner in range(owners):
            start = (part * owners + owner) * count
            out[owner, 0, part] = result[start : start + count]


def dft(volts, taps, parity, groups, owners):
    frames, inputs, length = volts.shape
    spec_count = frames - taps.shape[0] + 1
    half = length // 2
    coarse, fine = dft_tables(length, half, parity, groups)
    count = half // 2 // groups // owners
    width = inputs * spec_count
    group_rows = half // 2 // groups
    return pl.pallas_call(
        functools.partial(dft_kernel, parity, owners),
        grid=(groups,),
        in_specs=[WHOLE, WHOLE, pl.BlockSpec((1,) + coarse.shape[1:], lambda g: (g, 0, 0)), WHOLE],
        out_specs=pl.BlockSpec((owners, 1, 2, count, width), lambda g: (0, g, 0, 0, 0)),
        out_shape=jax.ShapeDtypeStruct((owners, groups, 2, count, width), jnp.bfloat16),
        scratch_shapes=[
            pltpu.VMEM((width, 128), jnp.float32),
            pltpu.VMEM((width, half), jnp.bfloat16),
            pltpu.VMEM((width, half), jnp.bfloat16),
            pltpu.VMEM((2 * group_rows, half), jnp.bfloat16),
            pltpu.VMEM((2 * group_rows, half), jnp.bfloat16),
        ],
        cost_estimate=pl.CostEstimate(
            flops=6 * half * half * width, bytes_accessed=2 * frames * inputs * length + 2 * half * width, transcendentals=0
        ),
    )(volts, taps, coarse, fine)


def correlate_kernel(sizes, got, out, scratch):
    cols, rows, groups, inputs = sizes
    sources, _, count, width = got.shape
    spec_count = width // inputs
    tiles = width // 128
    for part in range(2):
        for tile in range(tiles):
            value = got[:, part, :, tile * 128 : (tile + 1) * 128].astype(jnp.float32)
            scratch[part * tiles + tile] = value.reshape(sources * count, 128)

    def one_channel(k, carry):
        loaded = [scratch[x, pl.ds(k, sources, stride=count), :].astype(jnp.bfloat16) for x in range(2 * tiles)]
        each = tiles // inputs
        parts = [jnp.concatenate(loaded[x * each : (x + 1) * each], axis=1) for x in range(2 * inputs)]
        real, imag = parts[:inputs], parts[inputs:]
        left = jnp.concatenate([jnp.concatenate(x, axis=0) for x in (real, imag)], axis=1)
        near, far = [], []
        for col in range(cols):
            at = slice(col * rows * groups, (col + 1) * rows * groups)
            near += [x[at] for x in real] + [-x[at] for x in imag]
            far += [x[at] for x in imag] + [x[at] for x in real]
        right = jnp.concatenate([jnp.concatenate(near, axis=0), jnp.concatenate(far, axis=0)], axis=1)
        value = lax.dot_general(left, right, ROWS_ALIKE, preferred_element_type=jnp.float32) * (1.0 / spec_count)
        lanes = value.shape[1] // cols
        for row in range(rows):
            picked = jnp.concatenate(
                [value[(x * rows + row) * groups : (x * rows + row + 1) * groups] for x in range(inputs * cols)], axis=0
            ).astype(jnp.bfloat16)
            for col in range(cols):
                out[col * rows + row, k] = picked[:, col * lanes : (col + 1) * lanes]
        return carry

    lax.fori_loop(0, count, one_channel, 0)


def correlate(got, sizes):
    cols, rows, groups, inputs = sizes
    sources, _, count, width = got.shape
    block = groups * inputs
    shape = (cols * rows, count, cols * block, 2 * rows * block)
    return pl.pallas_call(
        functools.partial(correlate_kernel, sizes),
        in_specs=[WHOLE],
        out_specs=WHOLE,
        out_shape=jax.ShapeDtypeStruct(shape, jnp.bfloat16),
        scratch_shapes=[pltpu.VMEM((2 * width // 128, sources * count, 128), jnp.float32)],
        cost_estimate=pl.CostEstimate(
            flops=8 * count * sources * inputs * sources * width,
            bytes_accessed=2 * math.prod(got.shape) + 2 * math.prod(shape),
            transcendentals=0,
        ),
    )(got)


def finish_kernel(sizes, even, odd, place, out, scratch, held, sem):
    cols, rows, groups, inputs = sizes
    owners, count, width, lanes = even.shape
    tiles = lanes // 128
    for parity, got in enumerate((even, odd)):
        for tile in range(tiles):
            value = got[:, :, :, tile * 128 : (tile + 1) * 128].astype(jnp.float32)
            scratch[parity * tiles + tile] = value.reshape(owners * count * width, 128)

    def one_row(x, carry):
        i, rest = x // (cols * groups), x % (cols * groups)
        at = rest * inputs + i
        values = []
        for tile in range(tiles):
            pair = [scratch[p * tiles + tile, pl.ds(x, owners * count, stride=width), :] for p in range(2)]
            values.append(jnp.concatenate(pair, axis=0).T.astype(jnp.bfloat16))
        value = jnp.dot(jnp.concatenate(values, axis=0), place[...], preferred_element_type=jnp.float32)
        for part in range(2):
            for j in range(inputs):
                start = (part * inputs + j) * rows * groups
                first = part * rows * groups * inputs * width + j * width + at
                for half in range(held.shape[0]):
                    piece = value[start : start + rows * groups, half * 128 : (half + 1) * 128]
                    held[half, pl.ds(first, rows * groups, stride=inputs * width), :] = piece
        return carry

    lax.fori_loop(0, width, one_row, 0)
    copies = [
        pltpu.make_async_copy(held.at[half], out.at[:, pl.ds(half * 128, 128)], sem.at[half])
        for half in range(held.shape[0])
    ]
    for copy in copies:
        copy.start()
    for copy in copies:
        copy.wait()


def finish(even, odd, sizes):
    cols, rows, groups, inputs = sizes
    owners, count, width, lanes = even.shape
    channels = 2 * owners * count
    if channels % 128:
        value = jnp.stack([even, odd], axis=2).astype(jnp.float32)
        value = value.reshape(channels, inputs, cols, groups, 2, inputs, rows, groups)
        return value.transpose(4, 6, 7, 5, 2, 3, 1, 0).reshape(lanes * width, channels)
    source = np.arange(channels)
    target = source % (channels // 2) * 2 + source // (channels // 2)
    place = jnp.asarray(np.eye(channels)[target], jnp.bfloat16)
    return pl.pallas_call(
        functools.partial(finish_kernel, sizes),
        in_specs=[WHOLE] * 3,
        out_specs=pl.BlockSpec(memory_space=pl.ANY),
        out_shape=jax.ShapeDtypeStruct((lanes * width, channels), jnp.float32),
        scratch_shapes=[
            pltpu.VMEM((2 * lanes // 128, owners * count * width, 128), jnp.float32),
            pltpu.VMEM((channels // 128, lanes * width, 128), jnp.float32),
            pltpu.SemaphoreType.DMA((channels // 128,)),
        ],
    )(even, odd, place)


def shards(voltages, tap_table):
    groups, rows, cols = (lax.axis_size(name) for name in ("freq", "row", "col"))
    inputs = voltages.shape[0]
    sizes = (cols, rows, groups, inputs)
    volts = voltages.transpose(1, 0, 2)
    back = []
    for parity in range(2):
        sent = dft(volts, tap_table, parity, groups, rows * cols)
        sent = sent.reshape((-1,) + sent.shape[2:])
        got = lax.all_to_all(sent, EVERYONE, split_axis=0, concat_axis=0, tiled=True)
        back.append(lax.all_to_all(correlate(got, sizes), OWNERS, split_axis=0, concat_axis=0, tiled=True))
    result = finish(*back, sizes)
    block = groups * inputs
    return result.reshape(2, rows, block, cols * block, -1).transpose(4, 0, 1, 2, 3)


def solution(mesh):
    in_specs = (P(("row", "col", "freq"), None, None), P())
    out_specs = P("freq", None, None, "col", "row")
    return jax.shard_map(shards, mesh=mesh, in_specs=in_specs, out_specs=out_specs, check_vma=False)
```

```python
import functools
import math

import jax
import jax.numpy as jnp
import numpy as np
from jax import lax
from jax.experimental import pallas as pl
from jax.experimental.pallas import tpu as pltpu
from jax.sharding import PartitionSpec as P

OWNERS = ("col", "row")
EVERYONE = ("col", "row", "freq")
ROWS_ALIKE = (((1,), (1,)), ((), ()))
WHOLE = pl.BlockSpec(memory_space=pltpu.VMEM)

FOURS = (0, 4, ((1, 1, 1, 1),))
TWOS = (2, 4, ((1, -1, 1, -1),))
ODDS = (1, 2, ((1, 0, -1, 0), (0, 1, 0, -1)))
CHUNKS = ((FOURS,), (TWOS, ODDS))


def split(value):
    high = value.astype(jnp.bfloat16)
    low = (value - high.astype(jnp.float32)).astype(jnp.bfloat16)
    return high, low


def angle_tables(length, channels, kind):
    residue, modulus, folds = kind
    stride = 2 ** ((channels.bit_length() - 1) // 2)
    sample = np.arange(length // 4 * len(folds))
    factor = 1.0 / (64.0 * math.sqrt(length))
    coarse = 2.0 * math.pi / length * ((np.arange(0, channels, stride)[:, None] * sample) % length)
    fine = 2.0 * math.pi / length * ((np.arange(residue, stride, modulus)[:, None] * sample) % length)
    coarse = np.stack([np.cos(coarse), np.sin(coarse)]) * factor
    fine = np.stack([np.cos(fine), np.sin(fine)])
    return jnp.asarray(coarse, jnp.float32), jnp.asarray(fine, jnp.float32)


def signed_sum(values, signs):
    total = None
    for value, sign in zip(values, signs):
        if sign:
            total = value * sign if total is None else (total + value if sign > 0 else total - value)
    return total


def dft_kernel(kinds, volts, taps, *refs):
    tables, out, scratch = refs[: 2 * len(kinds)], refs[2 * len(kinds)], refs[2 * len(kinds) + 1 :]
    fold, scratch = scratch[0], scratch[1:]
    frames, inputs, length = volts.shape
    quarter = length // 4
    tap_count = taps.shape[0]
    spec_count = frames - tap_count + 1
    step, lanes = 8, 128
    rows = step * inputs
    for start in range(0, quarter, lanes):
        starts = [start + x * quarter for x in range(4)]
        weights = [taps[:, pl.ds(at, lanes)].astype(jnp.float32) / 4096.0 for at in starts]

        def filter_rows(index, carry):
            values = []
            for at, weight in zip(starts, weights):
                block = volts[pl.ds(index * step, step + tap_count - 1), :, pl.ds(at, lanes)].astype(jnp.float32)
                block = block.reshape(-1, lanes)
                value = weight[0:1] * block[:rows]
                for k in range(1, tap_count):
                    value = value + weight[k : k + 1] * block[k * inputs : k * inputs + rows]
                values.append(value)
            piece = 0
            for _, _, folds in kinds:
                for signs in folds:
                    fold[piece, pl.ds(pl.multiple_of(index * rows, rows), rows), :] = signed_sum(values, signs)
                    piece += 1
            return carry

        lax.fori_loop(0, spec_count // step, filter_rows, 0)
        piece = 0
        for x, (_, _, folds) in enumerate(kinds):
            high, low = scratch[4 * x : 4 * x + 2]
            for y in range(len(folds)):
                for i in range(inputs):
                    at = pl.ds(i * spec_count, spec_count), pl.ds(y * quarter + start, lanes)
                    high[at], low[at] = split(fold[piece, pl.ds(i, spec_count, stride=inputs), :])
                piece += 1

    dot = functools.partial(lax.dot_general, dimension_numbers=ROWS_ALIKE, preferred_element_type=jnp.float32)
    owners, groups, _, count, _ = out.shape
    slot = 0
    for x in range(len(kinds)):
        coarse, fine = tables[2 * x : 2 * x + 2]
        high, low, table_high, table_low = scratch[4 * x : 4 * x + 4]
        channels = table_high.shape[0] // 2
        fine_count = fine.shape[1]
        for a in range(channels // fine_count):
            cos_a, sin_a = coarse[0, a : a + 1], coarse[1, a : a + 1]
            real = cos_a * fine[0] - sin_a * fine[1]
            imag = -(sin_a * fine[0]) - cos_a * fine[1]
            for part, value in enumerate((real, imag)):
                at = pl.ds(part * channels + a * fine_count, fine_count)
                table_high[at], table_low[at] = split(value)
        result = dot(table_high[...], high[...]) + (dot(table_high[...], low[...]) + dot(table_low[...], high[...]))
        result = result.astype(jnp.bfloat16)
        each = channels // groups // owners
        for part in range(2):
            for group in range(groups):
                for owner in range(owners):
                    start = ((part * groups + group) * owners + owner) * each
                    out[owner, group, part, slot : slot + each] = result[start : start + each]
        slot += each


def dft(volts, taps, kinds, groups, owners):
    frames, inputs, length = volts.shape
    width = inputs * (frames - taps.shape[0] + 1)
    channels = length // 2
    operands, scratch, count, pieces, flops = [volts, taps], [], 0, 0, 0
    for kind in kinds:
        _, modulus, folds = kind
        operands += angle_tables(length, channels, kind)
        folded, rows = length // 4 * len(folds), 2 * channels // modulus
        scratch += [pltpu.VMEM((width, folded), jnp.bfloat16)] * 2 + [pltpu.VMEM((rows, folded), jnp.bfloat16)] * 2
        count += channels // modulus // groups // owners
        pieces += len(folds)
        flops += 6 * rows * folded * width
    shape = (owners, groups, 2, count, width)
    return pl.pallas_call(
        functools.partial(dft_kernel, kinds),
        in_specs=[WHOLE] * len(operands),
        out_specs=WHOLE,
        out_shape=jax.ShapeDtypeStruct(shape, jnp.bfloat16),
        scratch_shapes=[pltpu.VMEM((pieces, width, 128), jnp.float32)] + scratch,
        cost_estimate=pl.CostEstimate(
            flops=flops, bytes_accessed=2 * frames * inputs * length + 2 * math.prod(shape), transcendentals=0
        ),
    )(*operands)


def correlate_kernel(sizes, got, out, scratch):
    cols, rows, groups, inputs = sizes
    sources, _, count, width = got.shape
    spec_count = width // inputs
    tiles = width // 128
    for part in range(2):
        for tile in range(tiles):
            value = got[:, part, :, tile * 128 : (tile + 1) * 128].astype(jnp.float32)
            scratch[part * tiles + tile] = value.reshape(sources * count, 128)

    def one_channel(k, carry):
        loaded = [scratch[x, pl.ds(k, sources, stride=count), :].astype(jnp.bfloat16) for x in range(2 * tiles)]
        each = tiles // inputs
        parts = [jnp.concatenate(loaded[x * each : (x + 1) * each], axis=1) for x in range(2 * inputs)]
        real, imag = parts[:inputs], parts[inputs:]
        left = jnp.concatenate([jnp.concatenate(x, axis=0) for x in (real, imag)], axis=1)
        near, far = [], []
        for col in range(cols):
            at = slice(col * rows * groups, (col + 1) * rows * groups)
            near += [x[at] for x in real] + [-x[at] for x in imag]
            far += [x[at] for x in imag] + [x[at] for x in real]
        right = jnp.concatenate([jnp.concatenate(near, axis=0), jnp.concatenate(far, axis=0)], axis=1)
        value = lax.dot_general(left, right, ROWS_ALIKE, preferred_element_type=jnp.float32) * (1.0 / spec_count)
        lanes = value.shape[1] // cols
        for row in range(rows):
            picked = jnp.concatenate(
                [value[(x * rows + row) * groups : (x * rows + row + 1) * groups] for x in range(inputs * cols)], axis=0
            ).astype(jnp.bfloat16)
            for col in range(cols):
                out[col * rows + row, k] = picked[:, col * lanes : (col + 1) * lanes]
        return carry

    lax.fori_loop(0, count, one_channel, 0, unroll=2)


def correlate(got, sizes):
    cols, rows, groups, inputs = sizes
    sources, _, count, width = got.shape
    block = groups * inputs
    shape = (cols * rows, count, cols * block, 2 * rows * block)
    return pl.pallas_call(
        functools.partial(correlate_kernel, sizes),
        in_specs=[WHOLE],
        out_specs=WHOLE,
        out_shape=jax.ShapeDtypeStruct(shape, jnp.bfloat16),
        scratch_shapes=[pltpu.VMEM((2 * width // 128, sources * count, 128), jnp.float32)],
        cost_estimate=pl.CostEstimate(
            flops=8 * count * sources * inputs * sources * width,
            bytes_accessed=2 * math.prod(got.shape) + 2 * math.prod(shape),
            transcendentals=0,
        ),
    )(got)


def places(count_of):
    result = []
    for kinds in CHUNKS:
        result.append([residue + modulus * x for residue, modulus, _ in kinds for x in range(count_of(modulus))])
    return result


def finish_kernel(sizes, *refs):
    chunks, (same, out, scratch, held, sem) = refs[: len(CHUNKS)], refs[len(CHUNKS) :]
    cols, rows, groups, inputs = sizes
    owners, _, width, lanes = chunks[0].shape
    total = sum(got.shape[1] for got in chunks)
    tiles = lanes // 128
    for got, slots in zip(chunks, places(lambda modulus: total // modulus)):
        for owner in range(owners):
            for slot, place in enumerate(slots):
                for tile in range(tiles):
                    value = got[owner, slot, :, tile * 128 : (tile + 1) * 128].astype(jnp.float32)
                    scratch[tile, pl.ds((owner * total + place) * width, width), :] = value

    def one_row(x, carry):
        i, rest = x // (cols * groups), x % (cols * groups)
        at = rest * inputs + i
        for tile in range(tiles):
            block = scratch[tile, pl.ds(x, owners * total, stride=width), :].astype(jnp.bfloat16)
            value = lax.dot_general(same[...], block, ROWS_ALIKE, preferred_element_type=jnp.float32)
            for y in range(128 // (rows * groups)):
                first = (tile * (128 // (rows * groups)) + y)
                start = (first // inputs * rows * groups * inputs + first % inputs) * width + at
                for half in range(held.shape[0]):
                    piece = value[y * rows * groups : (y + 1) * rows * groups, half * 128 : (half + 1) * 128]
                    held[half, pl.ds(start, rows * groups, stride=inputs * width), :] = piece
        return carry

    lax.fori_loop(0, width, one_row, 0, unroll=4)
    copies = [
        pltpu.make_async_copy(held.at[half], out.at[:, pl.ds(half * 128, 128)], sem.at[half])
        for half in range(held.shape[0])
    ]
    for copy in copies:
        copy.start()
    for copy in copies:
        copy.wait()


def finish(chunks, sizes):
    cols, rows, groups, inputs = sizes
    owners, _, width, lanes = chunks[0].shape
    total = sum(got.shape[1] for got in chunks)
    channels = owners * total
    if channels % 128 or 128 % (rows * groups):
        order = np.argsort(sum(places(lambda modulus: total // modulus), []))
        value = jnp.concatenate(chunks, axis=1)[:, order].astype(jnp.float32)
        value = value.reshape(channels, inputs, cols, groups, 2, inputs, rows, groups)
        return value.transpose(4, 6, 7, 5, 2, 3, 1, 0).reshape(lanes * width, channels)
    return pl.pallas_call(
        functools.partial(finish_kernel, sizes),
        in_specs=[WHOLE] * (len(chunks) + 1),
        out_specs=pl.BlockSpec(memory_space=pl.ANY),
        out_shape=jax.ShapeDtypeStruct((lanes * width, channels), jnp.float32),
        scratch_shapes=[
            pltpu.VMEM((lanes // 128, channels * width, 128), jnp.float32),
            pltpu.VMEM((channels // 128, lanes * width, 128), jnp.float32),
            pltpu.SemaphoreType.DMA((channels // 128,)),
        ],
    )(*chunks, jnp.eye(128, dtype=jnp.bfloat16))


def shards(voltages, tap_table):
    groups, rows, cols = (lax.axis_size(name) for name in ("freq", "row", "col"))
    inputs = voltages.shape[0]
    sizes = (cols, rows, groups, inputs)
    volts = voltages.transpose(1, 0, 2)
    back = []
    for kinds in CHUNKS:
        sent = dft(volts, tap_table, kinds, groups, rows * cols)
        sent = sent.reshape((-1,) + sent.shape[2:])
        got = lax.all_to_all(sent, EVERYONE, split_axis=0, concat_axis=0, tiled=True)
        back.append(lax.all_to_all(correlate(got, sizes), OWNERS, split_axis=0, concat_axis=0, tiled=True))
    result = finish(back, sizes)
    block = groups * inputs
    return result.reshape(2, rows, block, cols * block, -1).transpose(4, 0, 1, 2, 3)


def solution(mesh):
    in_specs = (P(("row", "col", "freq"), None, None), P())
    out_specs = P("freq", None, None, "col", "row")
    return jax.shard_map(shards, mesh=mesh, in_specs=in_specs, out_specs=out_specs, check_vma=False)
```

```python
import functools
import math

import jax
import jax.numpy as jnp
import numpy as np
from jax import lax
from jax.experimental import pallas as pl
from jax.experimental.pallas import tpu as pltpu
from jax.sharding import PartitionSpec as P

OWNERS = ("col", "row")
EVERYONE = ("col", "row", "freq")
ROWS_ALIKE = (((1,), (1,)), ((), ()))
WHOLE = pl.BlockSpec(memory_space=pltpu.VMEM)

FOURS = (0, 4, ((1, 1, 1, 1),))
TWOS = (2, 4, ((1, -1, 1, -1),))
ODDS = (1, 2, ((1, 0, -1, 0), (0, 1, 0, -1)))
CHUNKS = ((FOURS,), (TWOS, ODDS))
PAD = 8


def split(value):
    high = value.astype(jnp.bfloat16)
    low = (value - high.astype(jnp.float32)).astype(jnp.bfloat16)
    return high, low


def angle_tables(length, channels, kind):
    residue, modulus, folds = kind
    stride = 2 ** ((channels.bit_length() - 1) // 2)
    sample = np.arange(length // 4 * len(folds))
    factor = 1.0 / (64.0 * math.sqrt(length))
    coarse = 2.0 * math.pi / length * ((np.arange(0, channels, stride)[:, None] * sample) % length)
    fine = 2.0 * math.pi / length * ((np.arange(residue, stride, modulus)[:, None] * sample) % length)
    coarse = np.stack([np.cos(coarse), np.sin(coarse)]) * factor
    fine = np.stack([np.cos(fine), np.sin(fine)])
    return jnp.asarray(coarse, jnp.float32), jnp.asarray(fine, jnp.float32)


def signed_sum(values, signs):
    total = None
    for value, sign in zip(values, signs):
        if sign:
            total = value * sign if total is None else (total + value if sign > 0 else total - value)
    return total


def dft_kernel(kinds, source, taps, *refs):
    tables, out, scratch = refs[: 2 * len(kinds)], refs[2 * len(kinds)], refs[2 * len(kinds) + 1 :]
    (volts, sem, fold), scratch = scratch[:3], scratch[3:]
    frames, inputs, length = volts.shape
    quarter = length // 4
    tap_count = taps.shape[0]
    spec_count = frames - tap_count + 1
    step, lanes, stages = 16, 128, sem.shape[0]
    rows, tiles = step * inputs, quarter // lanes
    bounds = [spec_count * x // stages + (tap_count - 1 if x else 0) for x in range(stages + 1)]
    copies = []
    for x in range(stages):
        part = pl.ds(bounds[x], bounds[x + 1] - bounds[x])
        copies.append(pltpu.make_async_copy(source.at[part], volts.at[part], sem.at[x]))
        copies[-1].start()

    def filter_rows(index, carry):
        for tile in range(tiles):
            values = []
            for x in range(4):
                at = pl.ds(x * quarter + tile * lanes, lanes)
                weight = taps[:, at].astype(jnp.float32) / 4096.0
                block = volts[pl.ds(index * step, step + tap_count - 1), :, at].astype(jnp.float32).reshape(-1, lanes)
                value = weight[0:1] * block[:rows]
                for k in range(1, tap_count):
                    value = value + weight[k : k + 1] * block[k * inputs : k * inputs + rows]
                values.append(value)
            piece = 0
            for _, _, folds in kinds:
                for signs in folds:
                    at = pl.ds(pl.multiple_of(index * rows, rows), rows)
                    fold[piece * tiles + tile, at, :] = signed_sum(values, signs)
                    piece += 1
        return carry

    for x in range(stages):
        copies[x].wait()
        lax.fori_loop(spec_count * x // stages // step, spec_count * (x + 1) // stages // step, filter_rows, 0)
    piece = 0
    for x, (_, _, folds) in enumerate(kinds):
        high, low = scratch[4 * x : 4 * x + 2]
        for y in range(len(folds)):
            for tile in range(tiles):
                for i in range(inputs):
                    at = pl.ds(i * spec_count, spec_count), pl.ds(y * quarter + tile * lanes, lanes)
                    high[at], low[at] = split(fold[piece, pl.ds(i, spec_count, stride=inputs), :])
                piece += 1

    dot = functools.partial(lax.dot_general, dimension_numbers=ROWS_ALIKE, preferred_element_type=jnp.float32)
    owners, groups, _, count, _ = out.shape
    slot = 0
    for x in range(len(kinds)):
        coarse, fine = tables[2 * x : 2 * x + 2]
        high, low, table_high, table_low = scratch[4 * x : 4 * x + 4]
        channels = table_high.shape[0] // 2
        fine_count = fine.shape[1]
        for a in range(channels // fine_count):
            cos_a, sin_a = coarse[0, a : a + 1], coarse[1, a : a + 1]
            real = cos_a * fine[0] - sin_a * fine[1]
            imag = -(sin_a * fine[0]) - cos_a * fine[1]
            for part, value in enumerate((real, imag)):
                at = pl.ds(part * channels + a * fine_count, fine_count)
                table_high[at], table_low[at] = split(value)
        result = dot(table_high[...], high[...]) + (dot(table_high[...], low[...]) + dot(table_low[...], high[...]))
        result = result.astype(jnp.bfloat16)
        each = channels // groups // owners
        for part in range(2):
            for group in range(groups):
                for owner in range(owners):
                    start = ((part * groups + group) * owners + owner) * each
                    out[owner, group, part, slot : slot + each] = result[start : start + each]
        slot += each


def dft(volts, taps, kinds, groups, owners):
    frames, inputs, length = volts.shape
    width = inputs * (frames - taps.shape[0] + 1)
    channels = length // 2
    operands, scratch, count, pieces, flops = [volts, taps], [], 0, 0, 0
    for kind in kinds:
        _, modulus, folds = kind
        operands += angle_tables(length, channels, kind)
        folded, rows = length // 4 * len(folds), 2 * channels // modulus
        scratch += [pltpu.VMEM((width, folded), jnp.bfloat16)] * 2 + [pltpu.VMEM((rows, folded), jnp.bfloat16)] * 2
        count += channels // modulus // groups // owners
        pieces += len(folds)
        flops += 6 * rows * folded * width
    shape = (owners, groups, 2, count, width)
    return pl.pallas_call(
        functools.partial(dft_kernel, kinds),
        in_specs=[pl.BlockSpec(memory_space=pl.ANY)] + [WHOLE] * (len(operands) - 1),
        out_specs=WHOLE,
        out_shape=jax.ShapeDtypeStruct(shape, jnp.bfloat16),
        scratch_shapes=[
            pltpu.VMEM(volts.shape, volts.dtype),
            pltpu.SemaphoreType.DMA((4,)),
            pltpu.VMEM((pieces * (length // 4 // 128), width, 128), jnp.float32),
            *scratch,
        ],
        cost_estimate=pl.CostEstimate(
            flops=flops, bytes_accessed=2 * frames * inputs * length + 2 * math.prod(shape), transcendentals=0
        ),
    )(*operands)


def correlate_kernel(sizes, me, got, *refs):
    outs, (scratch, out, sem) = refs[:-3], refs[-3:]
    cols, rows, groups, inputs = sizes
    sources, _, count, width = got.shape
    spec_count = width // inputs
    tiles = width // 128
    for part in range(2):
        for tile in range(tiles):
            value = got[:, part, :, tile * 128 : (tile + 1) * 128].astype(jnp.float32)
            scratch[part * tiles + tile] = value.reshape(sources * count, 128)

    def one_channel(k, carry):
        loaded = [scratch[x, pl.ds(k, sources, stride=count), :].astype(jnp.bfloat16) for x in range(2 * tiles)]
        each = tiles // inputs
        parts = [jnp.concatenate(loaded[x * each : (x + 1) * each], axis=1) for x in range(2 * inputs)]
        real, imag = parts[:inputs], parts[inputs:]
        left = jnp.concatenate([jnp.concatenate(x, axis=0) for x in (real, imag)], axis=1)
        near, far = [], []
        for col in range(cols):
            at = slice(col * rows * groups, (col + 1) * rows * groups)
            near += [x[at] for x in real] + [-x[at] for x in imag]
            far += [x[at] for x in imag] + [x[at] for x in real]
        right = jnp.concatenate([jnp.concatenate(near, axis=0), jnp.concatenate(far, axis=0)], axis=1)
        value = lax.dot_general(left, right, ROWS_ALIKE, preferred_element_type=jnp.float32) * (1.0 / spec_count)
        lanes = value.shape[1] // cols
        for row in range(rows):
            picked = jnp.concatenate(
                [value[(x * rows + row) * groups : (x * rows + row + 1) * groups] for x in range(inputs * cols)], axis=0
            ).astype(jnp.bfloat16)
            for col in range(cols):
                out[col * rows + row, k] = picked[:, col * lanes : (col + 1) * lanes]
        return carry

    lax.fori_loop(0, count, one_channel, 0, unroll=2)
    owners = cols * rows
    if len(outs) == 1:
        copies = [pltpu.make_async_copy(out, outs[0], sem.at[0])]
    else:
        copies = [pltpu.make_async_copy(out.at[lax.rem(me[0] + k, owners)], outs[k], sem.at[k]) for k in range(owners)]
    for copy in copies:
        copy.start()
    for copy in copies:
        copy.wait()


def correlate(got, me, sizes, apart):
    cols, rows, groups, inputs = sizes
    sources, _, count, width = got.shape
    block = groups * inputs
    shape = (cols * rows, count, cols * block, 2 * rows * block)
    return pl.pallas_call(
        functools.partial(correlate_kernel, sizes),
        in_specs=[pl.BlockSpec(memory_space=pltpu.SMEM), WHOLE],
        out_specs=[pl.BlockSpec(memory_space=pl.ANY)] * (shape[0] if apart else 1),
        out_shape=[jax.ShapeDtypeStruct(shape[1:] if apart else shape, jnp.bfloat16)] * (shape[0] if apart else 1),
        scratch_shapes=[
            pltpu.VMEM((2 * width // 128, sources * count, 128), jnp.float32),
            pltpu.VMEM(shape, jnp.bfloat16),
            pltpu.SemaphoreType.DMA((shape[0],)),
        ],
        cost_estimate=pl.CostEstimate(
            flops=8 * count * sources * inputs * sources * width,
            bytes_accessed=2 * math.prod(got.shape) + 2 * math.prod(shape),
            transcendentals=0,
        ),
    )(me, got)


def places(count_of):
    result = []
    for kinds in CHUNKS:
        result.append([residue + modulus * x for residue, modulus, _ in kinds for x in range(count_of(modulus))])
    return result


def finish_kernel(sizes, me, first, *refs):
    pieces, (same, out, scratch, held, sem) = refs[:-5], refs[-5:]
    cols, rows, groups, inputs = sizes
    owners, _, width, lanes = first.shape
    total = first.shape[1] + pieces[0].shape[0]
    tiles = lanes // 128
    pitch = scratch.shape[1] // (owners * total)
    whole = [(k, first.at[k], 0) for k in range(owners)]
    whole += [(lax.rem(me[0] + (owners - k), owners), piece, 1) for k, piece in enumerate(pieces)]
    slots_of = places(lambda modulus: total // modulus)
    for owner, got, chunk in whole:
        for slot, place in enumerate(slots_of[chunk]):
            for tile in range(tiles):
                value = got[slot, :, tile * 128 : (tile + 1) * 128].astype(jnp.float32)
                at = pl.multiple_of((owner * total + place) * pitch, 8)
                scratch[tile, pl.ds(at, width), :] = value

    flat = held.reshape(held.shape[0], held.shape[1] * held.shape[2], 128)

    copies = []
    for half in range(held.shape[0]):

        def one_row(x, carry):
            i, rest = x // (cols * groups), x % (cols * groups)
            at = rest * inputs + i
            for tile in range(tiles):
                rows_of = pl.ds(half * 128 * pitch + x, 128, stride=pitch)
                block = scratch[tile, rows_of, :].astype(jnp.bfloat16)
                value = lax.dot_general(same[...], block, ROWS_ALIKE, preferred_element_type=jnp.float32)
                for y in range(128 // (rows * groups)):
                    part, j = divmod(tile * (128 // (rows * groups)) + y, inputs)
                    start = part * rows * groups * held.shape[2] + j * width + at
                    piece = value[y * rows * groups : (y + 1) * rows * groups]
                    flat[half, pl.ds(start, rows * groups, stride=held.shape[2]), :] = piece
            return carry

        lax.fori_loop(0, width, one_row, 0, unroll=32)
        copies.append(
            pltpu.make_async_copy(
                held.at[half, :, pl.ds(0, out.shape[1])], out.at[:, :, pl.ds(half * 128, 128)], sem.at[half]
            )
        )
        copies[-1].start()
    for copy in copies:
        copy.wait()


def finish(first, pieces, me, sizes):
    cols, rows, groups, inputs = sizes
    owners, _, width, lanes = first.shape
    total = first.shape[1] + pieces[0].shape[0]
    channels = owners * total
    if channels % 128 or 128 % (rows * groups):
        order = np.argsort(sum(places(lambda modulus: total // modulus), []))
        second = jnp.stack(pieces)[(me[0] - jnp.arange(owners)) % owners]
        value = jnp.concatenate([first, second], axis=1)[:, order].astype(jnp.float32)
        value = value.reshape(channels, inputs, cols, groups, 2, inputs, rows, groups)
        return value.transpose(4, 6, 7, 5, 2, 3, 1, 0).reshape(lanes * width, channels)
    return pl.pallas_call(
        functools.partial(finish_kernel, sizes),
        in_specs=[pl.BlockSpec(memory_space=pltpu.SMEM)] + [WHOLE] * (owners + 2),
        out_specs=pl.BlockSpec(memory_space=pl.ANY),
        out_shape=jax.ShapeDtypeStruct((2 * rows * groups, inputs * width, channels), jnp.float32),
        scratch_shapes=[
            pltpu.VMEM((lanes // 128, channels * (width + PAD), 128), jnp.float32),
            pltpu.VMEM((channels // 128, 2 * rows * groups, inputs * width + PAD, 128), jnp.float32),
            pltpu.SemaphoreType.DMA((channels // 128,)),
        ],
    )(me, first, *pieces, jnp.eye(128, dtype=jnp.bfloat16))


def shards(voltages, tap_table):
    groups, rows, cols = (lax.axis_size(name) for name in ("freq", "row", "col"))
    inputs = voltages.shape[0]
    sizes = (cols, rows, groups, inputs)
    volts = voltages.transpose(1, 0, 2)
    owners = rows * cols
    me = lax.axis_index(OWNERS).astype(jnp.int32).reshape(1)
    got = []
    for kinds in CHUNKS:
        sent = dft(volts, tap_table, kinds, groups, owners)
        sent = sent.reshape((-1,) + sent.shape[2:])
        got.append(lax.all_to_all(sent, EVERYONE, split_axis=0, concat_axis=0, tiled=True))
    first = lax.all_to_all(correlate(got[0], me, sizes, False)[0], OWNERS, split_axis=0, concat_axis=0, tiled=True)
    pieces = list(correlate(got[1], me, sizes, True))
    meshed = lambda owner: owner % rows * cols + owner // rows
    for k in range(1, owners):
        pairs = [(meshed(x), meshed((x + k) % owners)) for x in range(owners)]
        pieces[k] = lax.ppermute(pieces[k], OWNERS[::-1], pairs)
    result = finish(first, pieces, me, sizes)
    block = groups * inputs
    return result.reshape(2, rows, block, cols * block, -1).transpose(4, 0, 1, 2, 3)


def solution(mesh):
    in_specs = (P(("row", "col", "freq"), None, None), P())
    out_specs = P("freq", None, None, "col", "row")
    return jax.shard_map(shards, mesh=mesh, in_specs=in_specs, out_specs=out_specs, check_vma=False)
```

```python
import functools
import math

import jax
import jax.numpy as jnp
import numpy as np
from jax import lax
from jax.experimental import pallas as pl
from jax.experimental.pallas import tpu as pltpu
from jax.sharding import PartitionSpec as P


OWNERS = ("col", "row")
EVERYONE = ("col", "row", "freq")
ROWS_ALIKE = (((1,), (1,)), ((), ()))
WHOLE = pl.BlockSpec(memory_space=pltpu.VMEM)
ANYWHERE = pl.BlockSpec(memory_space=pl.ANY)
SCALARS = pl.BlockSpec(memory_space=pltpu.SMEM)

FOURS = (0, 4, ((1, 1, 1, 1),))
TWOS = (2, 4, ((1, -1, 1, -1),))
ODDS = (1, 2, ((1, 0, -1, 0), (0, 1, 0, -1)))
CHUNKS = ((FOURS,), (TWOS, ODDS))
PAD = 8


def split(value):
    high = value.astype(jnp.bfloat16)
    low = (value - high.astype(jnp.float32)).astype(jnp.bfloat16)
    return high, low


def angle_tables(length, channels, kind):
    residue, modulus, folds = kind
    stride = 2 ** ((channels.bit_length() - 1) // 2)
    sample = np.arange(length // 4 * len(folds))
    factor = 1.0 / (64.0 * math.sqrt(length))
    coarse = 2.0 * math.pi / length * ((np.arange(0, channels, stride)[:, None] * sample) % length)
    fine = 2.0 * math.pi / length * ((np.arange(residue, stride, modulus)[:, None] * sample) % length)
    coarse = np.stack([np.cos(coarse), np.sin(coarse)]) * factor
    fine = np.stack([np.cos(fine), np.sin(fine)])
    return jnp.asarray(coarse, jnp.float32), jnp.asarray(fine, jnp.float32)


def signed_sum(values, signs):
    total = None
    for value, sign in zip(values, signs):
        if sign:
            total = value * sign if total is None else (total + value if sign > 0 else total - value)
    return total


def dft_kernel(kinds, rows_apart, me, source, taps, *refs):
    tables, outs, scratch = refs[: 2 * len(kinds)], refs[2 * len(kinds) :][: rows_apart or 1], refs[2 * len(kinds) :]
    out, volts, sem, fold = scratch[len(outs) : len(outs) + 4]
    scratch = scratch[len(outs) + 4 :]
    frames, inputs, length = volts.shape
    quarter = length // 4
    tap_count = taps.shape[0]
    spec_count = frames - tap_count + 1
    step, lanes, stages = 16, 128, sem.shape[0]
    rows, tiles = step * inputs, quarter // lanes
    bounds = [spec_count * x // stages + (tap_count - 1 if x else 0) for x in range(stages + 1)]
    copies = []
    for x in range(stages):
        part = pl.ds(bounds[x], bounds[x + 1] - bounds[x])
        copies.append(pltpu.make_async_copy(source.at[part], volts.at[part], sem.at[x, 0]))
        copies[-1].start()

    def filter_rows(index, carry):
        for tile in range(tiles):
            values = []
            for x in range(4):
                at = pl.ds(x * quarter + tile * lanes, lanes)
                weight = taps[:, at].astype(jnp.float32) / 4096.0
                block = volts[pl.ds(index * step, step + tap_count - 1), :, at].astype(jnp.float32).reshape(-1, lanes)
                value = weight[0:1] * block[:rows]
                for k in range(1, tap_count):
                    value = value + weight[k : k + 1] * block[k * inputs : k * inputs + rows]
                values.append(value)
            piece = 0
            for _, _, folds in kinds:
                for signs in folds:
                    at = pl.ds(pl.multiple_of(index * rows, rows), rows)
                    fold[piece * tiles + tile, at, :] = signed_sum(values, signs)
                    piece += 1
        return carry

    for x in range(stages):
        copies[x].wait()
        lax.fori_loop(spec_count * x // stages // step, spec_count * (x + 1) // stages // step, filter_rows, 0)
    piece = 0
    for x, (_, _, folds) in enumerate(kinds):
        high, low = scratch[4 * x : 4 * x + 2]
        for y in range(len(folds)):
            for tile in range(tiles):
                for i in range(inputs):
                    at = pl.ds(i * spec_count, spec_count), pl.ds(y * quarter + tile * lanes, lanes)
                    high[at], low[at] = split(fold[piece, pl.ds(i, spec_count, stride=inputs), :])
                piece += 1

    dot = functools.partial(lax.dot_general, dimension_numbers=ROWS_ALIKE, preferred_element_type=jnp.float32)
    owners, groups, _, _, _ = out.shape
    slot = 0
    for x in range(len(kinds)):
        coarse, fine = tables[2 * x : 2 * x + 2]
        high, low, table_high, table_low = scratch[4 * x : 4 * x + 4]
        channels = table_high.shape[0] // 2
        fine_count = fine.shape[1]
        for a in range(channels // fine_count):
            cos_a, sin_a = coarse[0, a : a + 1], coarse[1, a : a + 1]
            real = cos_a * fine[0] - sin_a * fine[1]
            imag = -(sin_a * fine[0]) - cos_a * fine[1]
            for part, value in enumerate((real, imag)):
                at = pl.ds(part * channels + a * fine_count, fine_count)
                table_high[at], table_low[at] = split(value)
        result = dot(table_high[...], high[...]) + (dot(table_high[...], low[...]) + dot(table_low[...], high[...]))
        result = result.astype(jnp.bfloat16)
        each = channels // groups // owners
        for part in range(2):
            for group in range(groups):
                for owner in range(owners):
                    start = ((part * groups + group) * owners + owner) * each
                    out[owner, group, part, slot : slot + each] = result[start : start + each]
        slot += each
    if rows_apart:
        row_of = [lax.rem(me[1] + k, rows_apart) for k in range(rows_apart)]
        copies = [
            pltpu.make_async_copy(out.at[pl.ds(col * rows_apart + row, 1)], outs[k].at[pl.ds(col, 1)], sem.at[k, col])
            for k, row in enumerate(row_of)
            for col in range(owners // rows_apart)
        ]
    else:
        copies = [pltpu.make_async_copy(out, outs[0], sem.at[0, 0])]
    for copy in copies:
        copy.start()
    for copy in copies:
        copy.wait()


def dft(volts, taps, me, kinds, groups, owners, rows_apart):
    frames, inputs, length = volts.shape
    width = inputs * (frames - taps.shape[0] + 1)
    channels = length // 2
    operands, scratch, count, pieces, flops = [me, volts, taps], [], 0, 0, 0
    for kind in kinds:
        _, modulus, folds = kind
        operands += angle_tables(length, channels, kind)
        folded, rows = length // 4 * len(folds), 2 * channels // modulus
        scratch += [pltpu.VMEM((width, folded), jnp.bfloat16)] * 2 + [pltpu.VMEM((rows, folded), jnp.bfloat16)] * 2
        count += channels // modulus // groups // owners
        pieces += len(folds)
        flops += 6 * rows * folded * width
    shape = (owners, groups, 2, count, width)
    out_shape = jax.ShapeDtypeStruct((owners // (rows_apart or 1),) + shape[1:] if rows_apart else shape, jnp.bfloat16)
    return pl.pallas_call(
        functools.partial(dft_kernel, kinds, rows_apart),
        in_specs=[SCALARS, ANYWHERE] + [WHOLE] * (len(operands) - 2),
        out_specs=[ANYWHERE] * (rows_apart or 1),
        out_shape=[out_shape] * (rows_apart or 1),
        scratch_shapes=[
            pltpu.VMEM(shape, jnp.bfloat16),
            pltpu.VMEM(volts.shape, volts.dtype),
            pltpu.SemaphoreType.DMA((4, owners)),
            pltpu.VMEM((pieces * (length // 4 // 128), width, 128), jnp.float32),
            *scratch,
        ],
        cost_estimate=pl.CostEstimate(
            flops=flops, bytes_accessed=2 * frames * inputs * length + 2 * math.prod(shape), transcendentals=0
        ),
    )(*operands)


def turn_kernel(me, *refs):
    sem = refs[-1]
    plane, rows = sem.shape
    blocks, outs = refs[:rows], refs[rows:-1]
    copies = []
    for q in range(plane):
        to = lax.rem(me[2] + q, plane)
        for k in range(rows):
            origin = lax.rem(me[1] + (rows - k), rows)
            copies.append(pltpu.make_async_copy(blocks[k].at[to], outs[q].at[origin], sem.at[q, k]))
    for copy in copies:
        copy.start()
    for copy in copies:
        copy.wait()


def turn(blocks, me):
    plane, rows = blocks[0].shape[0], len(blocks)
    shape = jax.ShapeDtypeStruct((rows,) + blocks[0].shape[1:], jnp.bfloat16)
    return pl.pallas_call(
        turn_kernel,
        in_specs=[SCALARS] + [WHOLE] * rows,
        out_specs=[ANYWHERE] * plane,
        out_shape=[shape] * plane,
        scratch_shapes=[pltpu.SemaphoreType.DMA((plane, rows))],
    )(me, *blocks)


def correlate_kernel(sizes, count, me, *refs):
    cols, rows, groups, inputs = sizes
    sources = cols * rows * groups
    out, scratch, sem = refs[-2], refs[-3], refs[-1]
    apart = refs[0].shape[0] == rows
    got, outs = (refs[: cols * groups], refs[cols * groups : -3]) if apart else (refs[0], refs[1:-3])
    width = scratch.shape[0] // 2 * 128
    spec_count = width // inputs
    tiles = width // 128
    for part in range(2):
        for tile in range(tiles):
            lanes = slice(tile * 128, (tile + 1) * 128)
            if not apart:
                scratch[part * tiles + tile] = got[:, part, :, lanes].astype(jnp.float32).reshape(sources * count, 128)
                continue
            for q, block in enumerate(got):
                origin = lax.rem(me[2] + (cols * groups - q), cols * groups)
                col, group = origin // groups, lax.rem(origin, groups)
                for row in range(rows):
                    at = pl.multiple_of(((col * rows + row) * groups + group) * count, 8)
                    scratch[part * tiles + tile, pl.ds(at, count), :] = block[row, part, :, lanes].astype(jnp.float32)

    def one_channel(k, carry):
        loaded = [scratch[x, pl.ds(k, sources, stride=count), :].astype(jnp.bfloat16) for x in range(2 * tiles)]
        each = tiles // inputs
        parts = [jnp.concatenate(loaded[x * each : (x + 1) * each], axis=1) for x in range(2 * inputs)]
        real, imag = parts[:inputs], parts[inputs:]
        left = jnp.concatenate([jnp.concatenate(x, axis=0) for x in (real, imag)], axis=1)
        near, far = [], []
        for col in range(cols):
            at = slice(col * rows * groups, (col + 1) * rows * groups)
            near += [x[at] for x in real] + [-x[at] for x in imag]
            far += [x[at] for x in imag] + [x[at] for x in real]
        right = jnp.concatenate([jnp.concatenate(near, axis=0), jnp.concatenate(far, axis=0)], axis=1)
        value = lax.dot_general(left, right, ROWS_ALIKE, preferred_element_type=jnp.float32) * (1.0 / spec_count)
        lanes = value.shape[1] // cols
        for row in range(rows):
            picked = jnp.concatenate(
                [value[(x * rows + row) * groups : (x * rows + row + 1) * groups] for x in range(inputs * cols)], axis=0
            ).astype(jnp.bfloat16)
            for col in range(cols):
                out[col * rows + row, k] = picked[:, col * lanes : (col + 1) * lanes]
        return carry

    lax.fori_loop(0, count, one_channel, 0, unroll=2)
    owners = cols * rows
    if len(outs) == 1:
        copies = [pltpu.make_async_copy(out, outs[0], sem.at[0])]
    else:
        copies = [pltpu.make_async_copy(out.at[lax.rem(me[0] + k, owners)], outs[k], sem.at[k]) for k in range(owners)]
    for copy in copies:
        copy.start()
    for copy in copies:
        copy.wait()


def correlate(got, me, sizes, apart):
    cols, rows, groups, inputs = sizes
    sources = cols * rows * groups
    count, width = got[0].shape[-2:]
    block = groups * inputs
    shape = (cols * rows, count, cols * block, 2 * rows * block)
    return pl.pallas_call(
        functools.partial(correlate_kernel, sizes, count),
        in_specs=[SCALARS] + [WHOLE] * len(got),
        out_specs=[pl.BlockSpec(memory_space=pl.ANY)] * (shape[0] if apart else 1),
        out_shape=[jax.ShapeDtypeStruct(shape[1:] if apart else shape, jnp.bfloat16)] * (shape[0] if apart else 1),
        scratch_shapes=[
            pltpu.VMEM((2 * width // 128, sources * count, 128), jnp.float32),
            pltpu.VMEM(shape, jnp.bfloat16),
            pltpu.SemaphoreType.DMA((shape[0],)),
        ],
        cost_estimate=pl.CostEstimate(
            flops=8 * count * sources * inputs * sources * width,
            bytes_accessed=4 * sources * count * width + 2 * math.prod(shape),
            transcendentals=0,
        ),
    )(me, *got)


def places(count_of):
    result = []
    for kinds in CHUNKS:
        result.append([residue + modulus * x for residue, modulus, _ in kinds for x in range(count_of(modulus))])
    return result


def finish_kernel(sizes, me, first, *refs):
    pieces, (same, out, scratch, held, sem) = refs[:-5], refs[-5:]
    cols, rows, groups, inputs = sizes
    owners, _, width, lanes = first.shape
    total = first.shape[1] + pieces[0].shape[0]
    tiles = lanes // 128
    pitch = scratch.shape[1] // (owners * total)
    whole = [(k, first.at[k], 0) for k in range(owners)]
    whole += [(lax.rem(me[0] + (owners - k), owners), piece, 1) for k, piece in enumerate(pieces)]
    slots_of = places(lambda modulus: total // modulus)
    for owner, got, chunk in whole:
        for slot, place in enumerate(slots_of[chunk]):
            for tile in range(tiles):
                value = got[slot, :, tile * 128 : (tile + 1) * 128].astype(jnp.float32)
                at = pl.multiple_of((owner * total + place) * pitch, 8)
                scratch[tile, pl.ds(at, width), :] = value

    flat = held.reshape(held.shape[0], held.shape[1] * held.shape[2], 128)

    copies = []
    for half in range(held.shape[0]):

        def one_row(x, carry):
            i, rest = x // (cols * groups), x % (cols * groups)
            at = rest * inputs + i
            for tile in range(tiles):
                rows_of = pl.ds(half * 128 * pitch + x, 128, stride=pitch)
                block = scratch[tile, rows_of, :].astype(jnp.bfloat16)
                value = lax.dot_general(same[...], block, ROWS_ALIKE, preferred_element_type=jnp.float32)
                for y in range(128 // (rows * groups)):
                    part, j = divmod(tile * (128 // (rows * groups)) + y, inputs)
                    start = part * rows * groups * held.shape[2] + j * width + at
                    piece = value[y * rows * groups : (y + 1) * rows * groups]
                    flat[half, pl.ds(start, rows * groups, stride=held.shape[2]), :] = piece
            return carry

        lax.fori_loop(0, width, one_row, 0, unroll=32)
        copies.append(
            pltpu.make_async_copy(
                held.at[half, :, pl.ds(0, out.shape[1])], out.at[:, :, pl.ds(half * 128, 128)], sem.at[half]
            )
        )
        copies[-1].start()
    for copy in copies:
        copy.wait()


def finish(first, pieces, me, sizes):
    cols, rows, groups, inputs = sizes
    owners, _, width, lanes = first.shape
    total = first.shape[1] + pieces[0].shape[0]
    channels = owners * total
    if channels % 128 or 128 % (rows * groups):
        order = np.argsort(sum(places(lambda modulus: total // modulus), []))
        second = jnp.stack(pieces)[(me[0] - jnp.arange(owners)) % owners]
        value = jnp.concatenate([first, second], axis=1)[:, order]
        value = value.reshape(channels, inputs, cols, groups, 2, inputs, rows, groups)
        return value.transpose(4, 6, 7, 5, 2, 3, 1, 0).reshape(lanes * width, channels).astype(jnp.float32)
    return pl.pallas_call(
        functools.partial(finish_kernel, sizes),
        in_specs=[pl.BlockSpec(memory_space=pltpu.SMEM)] + [WHOLE] * (owners + 2),
        out_specs=pl.BlockSpec(memory_space=pl.ANY),
        out_shape=jax.ShapeDtypeStruct((2 * rows * groups, inputs * width, channels), jnp.float32),
        scratch_shapes=[
            pltpu.VMEM((lanes // 128, channels * (width + PAD), 128), jnp.float32),
            pltpu.VMEM((channels // 128, 2 * rows * groups, inputs * width + PAD, 128), jnp.float32),
            pltpu.SemaphoreType.DMA((channels // 128,)),
        ],
    )(me, first, *pieces, jnp.eye(128, dtype=jnp.bfloat16))


def shards(voltages, tap_table):
    groups, rows, cols = (lax.axis_size(name) for name in ("freq", "row", "col"))
    inputs = voltages.shape[0]
    sizes = (cols, rows, groups, inputs)
    volts = voltages.transpose(1, 0, 2)
    owners = rows * cols
    plane = cols * groups
    row, col, group = (lax.axis_index(name) for name in ("row", "col", "freq"))
    me = jnp.stack([col * rows + row, row, col * groups + group]).astype(jnp.int32)

    blocks = list(dft(volts, tap_table, me, CHUNKS[0], groups, owners, rows))
    for k in range(1, rows):
        blocks[k] = lax.ppermute(blocks[k], "row", [(x, (x + k) % rows) for x in range(rows)])
    sent = dft(volts, tap_table, me, CHUNKS[1], groups, owners, 0)[0]
    sent = sent.reshape((-1,) + sent.shape[2:])
    second = lax.all_to_all(sent, EVERYONE, split_axis=0, concat_axis=0, tiled=True)
    blocks = list(turn([x.reshape((plane,) + x.shape[2:]) for x in blocks], me))
    meshed = lambda place: place % groups * cols + place // groups
    for q in range(1, plane):
        pairs = [(meshed(x), meshed((x + q) % plane)) for x in range(plane)]
        blocks[q] = lax.ppermute(blocks[q], ("freq", "col"), pairs)
    if blocks[0].shape[2] % 8:
        stacked = jnp.stack(blocks)[(me[2] - jnp.arange(plane)) % plane]
        stacked = stacked.reshape((cols, groups) + stacked.shape[1:]).swapaxes(1, 2)
        blocks = [stacked.reshape((-1,) + stacked.shape[3:])]

    first = correlate(blocks, me, sizes, False)[0]
    first = lax.all_to_all(first, OWNERS, split_axis=0, concat_axis=0, tiled=True)
    pieces = list(correlate([second], me, sizes, True))
    meshed = lambda owner: owner % rows * cols + owner // rows
    for k in range(1, owners):
        pairs = [(meshed(x), meshed((x + k) % owners)) for x in range(owners)]
        pieces[k] = lax.ppermute(pieces[k], OWNERS[::-1], pairs)
    result = finish(first, pieces, me, sizes)
    block = groups * inputs
    return result.reshape(2, rows, block, cols * block, -1).transpose(4, 0, 1, 2, 3)


def solution(mesh):
    in_specs = (P(("row", "col", "freq"), None, None), P())
    out_specs = P("freq", None, None, "col", "row")
    return jax.shard_map(shards, mesh=mesh, in_specs=in_specs, out_specs=out_specs, check_vma=False)
```

```python
import functools
import math

import jax
import jax.numpy as jnp
import numpy as np
from jax import lax
from jax.experimental import pallas as pl
from jax.experimental.pallas import tpu as pltpu
from jax.sharding import PartitionSpec as P


OWNERS = ("col", "row")
EVERYONE = ("col", "row", "freq")
ROWS_ALIKE = (((1,), (1,)), ((), ()))
WHOLE = pl.BlockSpec(memory_space=pltpu.VMEM)
ANYWHERE = pl.BlockSpec(memory_space=pl.ANY)
SCALARS = pl.BlockSpec(memory_space=pltpu.SMEM)

ROOT = math.sqrt(0.5)


def fours(x):
    return [(x[0] + x[4]) + (x[2] + x[6]), (x[1] + x[5]) + (x[3] + x[7])]


def twos(x):
    return [(x[0] + x[4]) - (x[2] + x[6]), (x[1] + x[5]) - (x[3] + x[7])]


def ones(x):
    turned = ((x[1] - x[5]) - (x[3] - x[7])) * ROOT, ((x[1] - x[5]) + (x[3] - x[7])) * ROOT
    return [(x[0] - x[4]) + turned[0], -(x[2] - x[6]) - turned[1]]


def fives(x):
    turned = ((x[1] - x[5]) - (x[3] - x[7])) * ROOT, ((x[1] - x[5]) + (x[3] - x[7])) * ROOT
    return [(x[0] - x[4]) - turned[0], turned[1] - (x[2] - x[6])]


FOURS = (4, {0: 0}, fours)
TWOS = (4, {2: 0}, twos)
ONES = (8, {1: 1, 7: -1}, ones)
FIVES = (8, {3: -1, 5: 1}, fives)
CHUNKS = ((FOURS,), (TWOS, ONES, FIVES))
PAD = 8


def split(value):
    high = value.astype(jnp.bfloat16)
    low = (value - high.astype(jnp.float32)).astype(jnp.bfloat16)
    return high, low


def places(kind, total):
    modulus, residues, _ = kind
    return [x for x in range(total) if x % modulus in residues]


def angle_tables(length, channels, kind):
    modulus, residues, _ = kind
    stride = 2 ** ((channels.bit_length() - 1) // 2)
    fine = np.array(places(kind, stride))
    signs = np.array([residues[x % modulus] for x in fine])
    sample = np.arange(length // 8 if signs.any() else length // 4)
    factor = 1.0 / (64.0 * math.sqrt(length))
    coarse = 2.0 * math.pi / length * ((np.arange(0, channels, stride)[:, None] * sample) % length)
    fine = 2.0 * math.pi / length * ((fine[:, None] * sample) % length)
    coarse = np.stack([np.cos(coarse), np.sin(coarse)]) * factor
    fine = np.stack([np.cos(fine), np.sin(fine), np.broadcast_to(signs[:, None], fine.shape)])
    return jnp.asarray(coarse, jnp.float32), jnp.asarray(fine, jnp.float32)


def dft_kernel(kinds, rows_apart, me, source, taps, *refs):
    tables, outs, scratch = refs[: 2 * len(kinds)], refs[2 * len(kinds) :][: rows_apart or 1], refs[2 * len(kinds) :]
    out, volts, sem, fold = scratch[len(outs) : len(outs) + 4]
    scratch = scratch[len(outs) + 4 :]
    frames, inputs, length = volts.shape
    eighth = length // 8
    tap_count = taps.shape[0]
    spec_count = frames - tap_count + 1
    step, lanes, stages = 16, 128, sem.shape[0]
    rows, tiles = step * inputs, eighth // lanes
    bounds = [spec_count * x // stages + (tap_count - 1 if x else 0) for x in range(stages + 1)]
    copies = []
    for x in range(stages):
        part = pl.ds(bounds[x], bounds[x + 1] - bounds[x])
        copies.append(pltpu.make_async_copy(source.at[part], volts.at[part], sem.at[x, 0]))
        copies[-1].start()

    def filter_rows(index, carry):
        for tile in range(tiles):
            values = []
            for x in range(8):
                at = pl.ds(x * eighth + tile * lanes, lanes)
                weight = taps[:, at].astype(jnp.float32) / 4096.0
                block = volts[pl.ds(index * step, step + tap_count - 1), :, at].astype(jnp.float32).reshape(-1, lanes)
                value = weight[0:1] * block[:rows]
                for k in range(1, tap_count):
                    value = value + weight[k : k + 1] * block[k * inputs : k * inputs + rows]
                values.append(value)
            piece = 0
            for _, _, folded in kinds:
                for value in folded(values):
                    fold[piece * tiles + tile, pl.ds(pl.multiple_of(index * rows, rows), rows), :] = value
                    piece += 1
        return carry

    for x in range(stages):
        copies[x].wait()
        lax.fori_loop(spec_count * x // stages // step, spec_count * (x + 1) // stages // step, filter_rows, 0)
    piece = 0
    for x in range(len(kinds)):
        high, low = scratch[4 * x : 4 * x + 2]
        for y in range(2):
            for tile in range(tiles):
                for i in range(inputs):
                    at = pl.ds(i * spec_count, spec_count), pl.ds(y * eighth + tile * lanes, lanes)
                    high[at], low[at] = split(fold[piece, pl.ds(i, spec_count, stride=inputs), :])
                piece += 1

    dot = functools.partial(lax.dot_general, dimension_numbers=ROWS_ALIKE, preferred_element_type=jnp.float32)
    owners, groups, _, _, _ = out.shape
    slot = 0
    for x in range(len(kinds)):
        coarse, fine = tables[2 * x : 2 * x + 2]
        high, low, table_high, table_low = scratch[4 * x : 4 * x + 4]
        channels = table_high.shape[0] // 2
        fine_count = fine.shape[1]
        for a in range(channels // fine_count):
            cos_a, sin_a = coarse[0, a : a + 1], coarse[1, a : a + 1]
            cosine = cos_a * fine[0] - sin_a * fine[1]
            sine = sin_a * fine[0] + cos_a * fine[1]
            values = [(cosine, -sine)]
            if cosine.shape[1] < table_high.shape[1]:
                values.append((sine * fine[2], cosine * fine[2]))
            for y, pair in enumerate(values):
                for part, value in enumerate(pair):
                    at = pl.ds(part * channels + a * fine_count, fine_count), pl.ds(y * eighth, value.shape[1])
                    table_high[at], table_low[at] = split(value)
        result = dot(table_high[...], high[...]) + (dot(table_high[...], low[...]) + dot(table_low[...], high[...]))
        result = result.astype(jnp.bfloat16)
        each = channels // groups // owners
        for part in range(2):
            for group in range(groups):
                for owner in range(owners):
                    start = ((part * groups + group) * owners + owner) * each
                    out[owner, group, part, slot : slot + each] = result[start : start + each]
        slot += each
    if rows_apart:
        row_of = [lax.rem(me[1] + k, rows_apart) for k in range(rows_apart)]
        copies = [
            pltpu.make_async_copy(out.at[pl.ds(col * rows_apart + row, 1)], outs[k].at[pl.ds(col, 1)], sem.at[k, col])
            for k, row in enumerate(row_of)
            for col in range(owners // rows_apart)
        ]
    else:
        copies = [pltpu.make_async_copy(out, outs[0], sem.at[0, 0])]
    for copy in copies:
        copy.start()
    for copy in copies:
        copy.wait()


def dft(volts, taps, me, kinds, groups, owners, rows_apart):
    frames, inputs, length = volts.shape
    width = inputs * (frames - taps.shape[0] + 1)
    channels = length // 2
    operands, scratch, count, pieces, flops = [me, volts, taps], [], 0, 0, 0
    for kind in kinds:
        operands += angle_tables(length, channels, kind)
        folded, rows = length // 4, 2 * len(places(kind, channels))
        scratch += [pltpu.VMEM((width, folded), jnp.bfloat16)] * 2 + [pltpu.VMEM((rows, folded), jnp.bfloat16)] * 2
        count += rows // 2 // groups // owners
        pieces += 2
        flops += 6 * rows * folded * width
    shape = (owners, groups, 2, count, width)
    out_shape = jax.ShapeDtypeStruct((owners // (rows_apart or 1),) + shape[1:] if rows_apart else shape, jnp.bfloat16)
    return pl.pallas_call(
        functools.partial(dft_kernel, kinds, rows_apart),
        in_specs=[SCALARS, ANYWHERE] + [WHOLE] * (len(operands) - 2),
        out_specs=[ANYWHERE] * (rows_apart or 1),
        out_shape=[out_shape] * (rows_apart or 1),
        scratch_shapes=[
            pltpu.VMEM(shape, jnp.bfloat16),
            pltpu.VMEM(volts.shape, volts.dtype),
            pltpu.SemaphoreType.DMA((4, owners)),
            pltpu.VMEM((pieces * (length // 8 // 128), width, 128), jnp.float32),
            *scratch,
        ],
        cost_estimate=pl.CostEstimate(
            flops=flops, bytes_accessed=2 * frames * inputs * length + 2 * math.prod(shape), transcendentals=0
        ),
    )(*operands)


def turn_kernel(me, *refs):
    sem = refs[-1]
    plane, rows = sem.shape
    blocks, outs = refs[:rows], refs[rows:-1]
    copies = []
    for q in range(plane):
        to = lax.rem(me[2] + q, plane)
        for k in range(rows):
            origin = lax.rem(me[1] + (rows - k), rows)
            copies.append(pltpu.make_async_copy(blocks[k].at[to], outs[q].at[origin], sem.at[q, k]))
    for copy in copies:
        copy.start()
    for copy in copies:
        copy.wait()


def turn(blocks, me):
    plane, rows = blocks[0].shape[0], len(blocks)
    shape = jax.ShapeDtypeStruct((rows,) + blocks[0].shape[1:], jnp.bfloat16)
    return pl.pallas_call(
        turn_kernel,
        in_specs=[SCALARS] + [WHOLE] * rows,
        out_specs=[ANYWHERE] * plane,
        out_shape=[shape] * plane,
        scratch_shapes=[pltpu.SemaphoreType.DMA((plane, rows))],
    )(me, *blocks)


def correlate_kernel(sizes, count, me, *refs):
    cols, rows, groups, inputs = sizes
    sources = cols * rows * groups
    out, scratch, sem = refs[-2], refs[-3], refs[-1]
    apart = refs[0].shape[0] == rows
    got, outs = (refs[: cols * groups], refs[cols * groups : -3]) if apart else (refs[0], refs[1:-3])
    width = scratch.shape[0] // 2 * 128
    spec_count = width // inputs
    tiles = width // 128
    for part in range(2):
        for tile in range(tiles):
            lanes = slice(tile * 128, (tile + 1) * 128)
            if not apart:
                scratch[part * tiles + tile] = got[:, part, :, lanes].astype(jnp.float32).reshape(sources * count, 128)
                continue
            for q, block in enumerate(got):
                origin = lax.rem(me[2] + (cols * groups - q), cols * groups)
                col, group = origin // groups, lax.rem(origin, groups)
                for row in range(rows):
                    at = pl.multiple_of(((col * rows + row) * groups + group) * count, 8)
                    scratch[part * tiles + tile, pl.ds(at, count), :] = block[row, part, :, lanes].astype(jnp.float32)

    def one_channel(k, carry):
        loaded = [scratch[x, pl.ds(k, sources, stride=count), :].astype(jnp.bfloat16) for x in range(2 * tiles)]
        each = tiles // inputs
        parts = [jnp.concatenate(loaded[x * each : (x + 1) * each], axis=1) for x in range(2 * inputs)]
        real, imag = parts[:inputs], parts[inputs:]
        left = jnp.concatenate([jnp.concatenate(x, axis=0) for x in (real, imag)], axis=1)
        near, far = [], []
        for col in range(cols):
            at = slice(col * rows * groups, (col + 1) * rows * groups)
            near += [x[at] for x in real] + [-x[at] for x in imag]
            far += [x[at] for x in imag] + [x[at] for x in real]
        right = jnp.concatenate([jnp.concatenate(near, axis=0), jnp.concatenate(far, axis=0)], axis=1)
        value = lax.dot_general(left, right, ROWS_ALIKE, preferred_element_type=jnp.float32) * (1.0 / spec_count)
        lanes = value.shape[1] // cols
        for row in range(rows):
            picked = jnp.concatenate(
                [value[(x * rows + row) * groups : (x * rows + row + 1) * groups] for x in range(inputs * cols)], axis=0
            ).astype(jnp.bfloat16)
            for col in range(cols):
                out[col * rows + row, k] = picked[:, col * lanes : (col + 1) * lanes]
        return carry

    lax.fori_loop(0, count, one_channel, 0, unroll=2)
    owners = cols * rows
    if len(outs) == 1:
        copies = [pltpu.make_async_copy(out, outs[0], sem.at[0])]
    else:
        copies = [pltpu.make_async_copy(out.at[lax.rem(me[0] + k, owners)], outs[k], sem.at[k]) for k in range(owners)]
    for copy in copies:
        copy.start()
    for copy in copies:
        copy.wait()


def correlate(got, me, sizes, apart):
    cols, rows, groups, inputs = sizes
    sources = cols * rows * groups
    count, width = got[0].shape[-2:]
    block = groups * inputs
    shape = (cols * rows, count, cols * block, 2 * rows * block)
    return pl.pallas_call(
        functools.partial(correlate_kernel, sizes, count),
        in_specs=[SCALARS] + [WHOLE] * len(got),
        out_specs=[pl.BlockSpec(memory_space=pl.ANY)] * (shape[0] if apart else 1),
        out_shape=[jax.ShapeDtypeStruct(shape[1:] if apart else shape, jnp.bfloat16)] * (shape[0] if apart else 1),
        scratch_shapes=[
            pltpu.VMEM((2 * width // 128, sources * count, 128), jnp.float32),
            pltpu.VMEM(shape, jnp.bfloat16),
            pltpu.SemaphoreType.DMA((shape[0],)),
        ],
        cost_estimate=pl.CostEstimate(
            flops=8 * count * sources * inputs * sources * width,
            bytes_accessed=4 * sources * count * width + 2 * math.prod(shape),
            transcendentals=0,
        ),
    )(me, *got)


def finish_kernel(sizes, me, first, *refs):
    pieces, (same, out, scratch, held, sem) = refs[:-5], refs[-5:]
    cols, rows, groups, inputs = sizes
    owners, _, width, lanes = first.shape
    total = first.shape[1] + pieces[0].shape[0]
    tiles = lanes // 128
    pitch = scratch.shape[1] // (owners * total)
    whole = [(k, first.at[k], 0) for k in range(owners)]
    whole += [(lax.rem(me[0] + (owners - k), owners), piece, 1) for k, piece in enumerate(pieces)]
    slots_of = [sum((places(kind, total) for kind in kinds), []) for kinds in CHUNKS]
    for owner, got, chunk in whole:
        for slot, place in enumerate(slots_of[chunk]):
            for tile in range(tiles):
                value = got[slot, :, tile * 128 : (tile + 1) * 128].astype(jnp.float32)
                at = pl.multiple_of((owner * total + place) * pitch, 8)
                scratch[tile, pl.ds(at, width), :] = value

    flat = held.reshape(held.shape[0], held.shape[1] * held.shape[2], 128)

    copies = []
    for half in range(held.shape[0]):

        def one_row(x, carry):
            i, rest = x // (cols * groups), x % (cols * groups)
            at = rest * inputs + i
            for tile in range(tiles):
                rows_of = pl.ds(half * 128 * pitch + x, 128, stride=pitch)
                block = scratch[tile, rows_of, :].astype(jnp.bfloat16)
                value = lax.dot_general(same[...], block, ROWS_ALIKE, preferred_element_type=jnp.float32)
                for y in range(128 // (rows * groups)):
                    part, j = divmod(tile * (128 // (rows * groups)) + y, inputs)
                    start = part * rows * groups * held.shape[2] + j * width + at
                    piece = value[y * rows * groups : (y + 1) * rows * groups]
                    flat[half, pl.ds(start, rows * groups, stride=held.shape[2]), :] = piece
            return carry

        lax.fori_loop(0, width, one_row, 0, unroll=32)
        copies.append(
            pltpu.make_async_copy(
                held.at[half, :, pl.ds(0, out.shape[1])], out.at[:, :, pl.ds(half * 128, 128)], sem.at[half]
            )
        )
        copies[-1].start()
    for copy in copies:
        copy.wait()


def finish(first, pieces, me, sizes):
    cols, rows, groups, inputs = sizes
    owners, _, width, lanes = first.shape
    total = first.shape[1] + pieces[0].shape[0]
    channels = owners * total
    if channels % 128 or 128 % (rows * groups):
        order = np.argsort(sum((places(kind, total) for kinds in CHUNKS for kind in kinds), []))
        second = jnp.stack(pieces)[(me[0] - jnp.arange(owners)) % owners]
        value = jnp.concatenate([first, second], axis=1)[:, order]
        value = value.reshape(channels, inputs, cols, groups, 2, inputs, rows, groups)
        return value.transpose(4, 6, 7, 5, 2, 3, 1, 0).reshape(lanes * width, channels).astype(jnp.float32)
    return pl.pallas_call(
        functools.partial(finish_kernel, sizes),
        in_specs=[pl.BlockSpec(memory_space=pltpu.SMEM)] + [WHOLE] * (owners + 2),
        out_specs=pl.BlockSpec(memory_space=pl.ANY),
        out_shape=jax.ShapeDtypeStruct((2 * rows * groups, inputs * width, channels), jnp.float32),
        scratch_shapes=[
            pltpu.VMEM((lanes // 128, channels * (width + PAD), 128), jnp.float32),
            pltpu.VMEM((channels // 128, 2 * rows * groups, inputs * width + PAD, 128), jnp.float32),
            pltpu.SemaphoreType.DMA((channels // 128,)),
        ],
    )(me, first, *pieces, jnp.eye(128, dtype=jnp.bfloat16))


def shards(voltages, tap_table):
    groups, rows, cols = (lax.axis_size(name) for name in ("freq", "row", "col"))
    inputs = voltages.shape[0]
    sizes = (cols, rows, groups, inputs)
    volts = voltages.transpose(1, 0, 2)
    owners = rows * cols
    plane = cols * groups
    row, col, group = (lax.axis_index(name) for name in ("row", "col", "freq"))
    me = jnp.stack([col * rows + row, row, col * groups + group]).astype(jnp.int32)

    blocks = list(dft(volts, tap_table, me, CHUNKS[0], groups, owners, rows))
    for k in range(1, rows):
        blocks[k] = lax.ppermute(blocks[k], "row", [(x, (x + k) % rows) for x in range(rows)])
    sent = dft(volts, tap_table, me, CHUNKS[1], groups, owners, 0)[0]
    sent = sent.reshape((-1,) + sent.shape[2:])
    second = lax.all_to_all(sent, EVERYONE, split_axis=0, concat_axis=0, tiled=True)
    blocks = list(turn([x.reshape((plane,) + x.shape[2:]) for x in blocks], me))
    meshed = lambda place: place % groups * cols + place // groups
    for q in range(1, plane):
        pairs = [(meshed(x), meshed((x + q) % plane)) for x in range(plane)]
        blocks[q] = lax.ppermute(blocks[q], ("freq", "col"), pairs)
    if blocks[0].shape[2] % 8:
        stacked = jnp.stack(blocks)[(me[2] - jnp.arange(plane)) % plane]
        stacked = stacked.reshape((cols, groups) + stacked.shape[1:]).swapaxes(1, 2)
        blocks = [stacked.reshape((-1,) + stacked.shape[3:])]

    first = correlate(blocks, me, sizes, False)[0]
    first = lax.all_to_all(first, OWNERS, split_axis=0, concat_axis=0, tiled=True)
    pieces = list(correlate([second], me, sizes, True))
    meshed = lambda owner: owner % rows * cols + owner // rows
    for k in range(1, owners):
        pairs = [(meshed(x), meshed((x + k) % owners)) for x in range(owners)]
        pieces[k] = lax.ppermute(pieces[k], OWNERS[::-1], pairs)
    result = finish(first, pieces, me, sizes)
    block = groups * inputs
    return result.reshape(2, rows, block, cols * block, -1).transpose(4, 0, 1, 2, 3)


def solution(mesh):
    in_specs = (P(("row", "col", "freq"), None, None), P())
    out_specs = P("freq", None, None, "col", "row")
    return jax.shard_map(shards, mesh=mesh, in_specs=in_specs, out_specs=out_specs, check_vma=False)
```

```python
import functools
import math

import jax
import jax.numpy as jnp
import numpy as np
from jax import lax
from jax.experimental import pallas as pl
from jax.experimental.pallas import tpu as pltpu
from jax.sharding import PartitionSpec as P


OWNERS = ("col", "row")
EVERYONE = ("col", "row", "freq")
ROWS_ALIKE = (((1,), (1,)), ((), ()))
WHOLE = pl.BlockSpec(memory_space=pltpu.VMEM)
ANYWHERE = pl.BlockSpec(memory_space=pl.ANY)

ROOT = math.sqrt(0.5)


def fours(x):
    return [(x[0] + x[4]) + (x[2] + x[6]), (x[1] + x[5]) + (x[3] + x[7])]


def twos(x):
    return [(x[0] + x[4]) - (x[2] + x[6]), (x[1] + x[5]) - (x[3] + x[7])]


def ones(x):
    turned = ((x[1] - x[5]) - (x[3] - x[7])) * ROOT, ((x[1] - x[5]) + (x[3] - x[7])) * ROOT
    return [(x[0] - x[4]) + turned[0], -(x[2] - x[6]) - turned[1]]


def fives(x):
    turned = ((x[1] - x[5]) - (x[3] - x[7])) * ROOT, ((x[1] - x[5]) + (x[3] - x[7])) * ROOT
    return [(x[0] - x[4]) - turned[0], turned[1] - (x[2] - x[6])]


FOURS = (4, {0: 0}, fours)
TWOS = (4, {2: 0}, twos)
ONES = (8, {1: 1, 7: -1}, ones)
FIVES = (8, {3: -1, 5: 1}, fives)
CHUNKS = ((FOURS,), (TWOS, ONES, FIVES))
PAD = 8


def position():
    row, col, group = (lax.axis_index(name) for name in ("row", "col", "freq"))
    return col * lax.axis_size("row") + row, row, col * lax.axis_size("freq") + group


def split(value):
    high = value.astype(jnp.bfloat16)
    low = (value - high.astype(jnp.float32)).astype(jnp.bfloat16)
    return high, low


def places(kind, total):
    modulus, residues, _ = kind
    return [x for x in range(total) if x % modulus in residues]


def angle_tables(length, channels, kind):
    modulus, residues, _ = kind
    stride = 2 ** ((channels.bit_length() - 1) // 2)
    fine = np.array(places(kind, stride))
    signs = np.array([residues[x % modulus] for x in fine])
    sample = np.arange(length // 8 if signs.any() else length // 4)
    factor = 1.0 / (64.0 * math.sqrt(length))
    coarse = 2.0 * math.pi / length * ((np.arange(0, channels, stride)[:, None] * sample) % length)
    fine = 2.0 * math.pi / length * ((fine[:, None] * sample) % length)
    coarse = np.stack([np.cos(coarse), np.sin(coarse)]) * factor
    fine = np.stack([np.cos(fine), np.sin(fine), np.broadcast_to(signs[:, None], fine.shape)])
    return jnp.asarray(coarse, jnp.float32), jnp.asarray(fine, jnp.float32)


def dft_kernel(kinds, rows_apart, source, taps, *refs):
    me = position()
    tables, outs, scratch = refs[: 2 * len(kinds)], refs[2 * len(kinds) :][: rows_apart or 1], refs[2 * len(kinds) :]
    out, volts, sem, fold = scratch[len(outs) : len(outs) + 4]
    scratch = scratch[len(outs) + 4 :]
    frames, inputs, length = volts.shape
    eighth = length // 8
    tap_count = taps.shape[0]
    spec_count = frames - tap_count + 1
    step, lanes, stages = 32, 128, sem.shape[0]
    rows, tiles = step * inputs, eighth // lanes
    bounds = [spec_count * x // stages + (tap_count - 1 if x else 0) for x in range(stages + 1)]
    copies = []
    for x in range(stages):
        part = pl.ds(bounds[x], bounds[x + 1] - bounds[x])
        copies.append(pltpu.make_async_copy(source.at[part], volts.at[part], sem.at[x, 0]))
        copies[-1].start()

    def filter_rows(index, carry):
        for tile in range(tiles):
            values = []
            for x in range(8):
                at = pl.ds(x * eighth + tile * lanes, lanes)
                weight = taps[:, at].astype(jnp.float32) / 4096.0
                block = volts[pl.ds(index * step, step + tap_count - 1), :, at].astype(jnp.float32).reshape(-1, lanes)
                value = weight[0:1] * block[:rows]
                for k in range(1, tap_count):
                    value = value + weight[k : k + 1] * block[k * inputs : k * inputs + rows]
                values.append(value)
            piece = 0
            for _, _, folded in kinds:
                for value in folded(values):
                    fold[piece * tiles + tile, pl.ds(pl.multiple_of(index * rows, rows), rows), :] = value
                    piece += 1
        return carry

    for x in range(stages):
        copies[x].wait()
        lax.fori_loop(spec_count * x // stages // step, spec_count * (x + 1) // stages // step, filter_rows, 0)
    piece = 0
    for x in range(len(kinds)):
        high, low = scratch[4 * x : 4 * x + 2]
        for y in range(2):
            for tile in range(tiles):
                for i in range(inputs):
                    at = pl.ds(i * spec_count, spec_count), pl.ds(y * eighth + tile * lanes, lanes)
                    high[at], low[at] = split(fold[piece, pl.ds(i, spec_count, stride=inputs), :])
                piece += 1

    dot = functools.partial(lax.dot_general, dimension_numbers=ROWS_ALIKE, preferred_element_type=jnp.float32)
    owners, groups, _, _, _ = out.shape
    slot = 0
    for x in range(len(kinds)):
        coarse, fine = tables[2 * x : 2 * x + 2]
        high, low, table_high, table_low = scratch[4 * x : 4 * x + 4]
        channels = table_high.shape[0] // 2
        fine_count = fine.shape[1]
        for a in range(channels // fine_count):
            cos_a, sin_a = coarse[0, a : a + 1], coarse[1, a : a + 1]
            cosine = cos_a * fine[0] - sin_a * fine[1]
            sine = sin_a * fine[0] + cos_a * fine[1]
            values = [(cosine, -sine)]
            if cosine.shape[1] < table_high.shape[1]:
                values.append((sine * fine[2], cosine * fine[2]))
            for y, pair in enumerate(values):
                for part, value in enumerate(pair):
                    at = pl.ds(part * channels + a * fine_count, fine_count), pl.ds(y * eighth, value.shape[1])
                    table_high[at], table_low[at] = split(value)
        result = dot(table_high[...], high[...]) + (dot(table_high[...], low[...]) + dot(table_low[...], high[...]))
        result = result.astype(jnp.bfloat16)
        each = channels // groups // owners
        for part in range(2):
            for group in range(groups):
                for owner in range(owners):
                    start = ((part * groups + group) * owners + owner) * each
                    out[owner, group, part, slot : slot + each] = result[start : start + each]
        slot += each
    if rows_apart:
        row_of = [lax.rem(me[1] + k, rows_apart) for k in range(rows_apart)]
        copies = [
            pltpu.make_async_copy(out.at[pl.ds(col * rows_apart + row, 1)], outs[k].at[pl.ds(col, 1)], sem.at[k, col])
            for k, row in enumerate(row_of)
            for col in range(owners // rows_apart)
        ]
    else:
        copies = [pltpu.make_async_copy(out, outs[0], sem.at[0, 0])]
    for copy in copies:
        copy.start()
    for copy in copies:
        copy.wait()


def dft(volts, taps, kinds, groups, owners, rows_apart):
    frames, inputs, length = volts.shape
    width = inputs * (frames - taps.shape[0] + 1)
    channels = length // 2
    operands, scratch, count, pieces, flops = [volts, taps], [], 0, 0, 0
    for kind in kinds:
        operands += angle_tables(length, channels, kind)
        folded, rows = length // 4, 2 * len(places(kind, channels))
        scratch += [pltpu.VMEM((width, folded), jnp.bfloat16)] * 2 + [pltpu.VMEM((rows, folded), jnp.bfloat16)] * 2
        count += rows // 2 // groups // owners
        pieces += 2
        flops += 6 * rows * folded * width
    shape = (owners, groups, 2, count, width)
    out_shape = jax.ShapeDtypeStruct((owners // (rows_apart or 1),) + shape[1:] if rows_apart else shape, jnp.bfloat16)
    return pl.pallas_call(
        functools.partial(dft_kernel, kinds, rows_apart),
        in_specs=[ANYWHERE] + [WHOLE] * (len(operands) - 1),
        out_specs=[ANYWHERE] * (rows_apart or 1),
        out_shape=[out_shape] * (rows_apart or 1),
        scratch_shapes=[
            pltpu.VMEM(shape, jnp.bfloat16),
            pltpu.VMEM(volts.shape, volts.dtype),
            pltpu.SemaphoreType.DMA((4, owners)),
            pltpu.VMEM((pieces * (length // 8 // 128), width, 128), jnp.float32),
            *scratch,
        ],
        cost_estimate=pl.CostEstimate(
            flops=flops, bytes_accessed=2 * frames * inputs * length + 2 * math.prod(shape), transcendentals=0
        ),
    )(*operands)


def turn_kernel(*refs):
    me = position()
    sem = refs[-1]
    plane, rows = sem.shape
    blocks, outs = refs[:rows], refs[rows:-1]
    copies = []
    for q in range(plane):
        to = lax.rem(me[2] + q, plane)
        for k in range(rows):
            origin = lax.rem(me[1] + (rows - k), rows)
            copies.append(pltpu.make_async_copy(blocks[k].at[to], outs[q].at[origin], sem.at[q, k]))
    for copy in copies:
        copy.start()
    for copy in copies:
        copy.wait()


def turn(blocks):
    plane, rows = blocks[0].shape[0], len(blocks)
    shape = jax.ShapeDtypeStruct((rows,) + blocks[0].shape[1:], jnp.bfloat16)
    return pl.pallas_call(
        turn_kernel,
        in_specs=[WHOLE] * rows,
        out_specs=[ANYWHERE] * plane,
        out_shape=[shape] * plane,
        scratch_shapes=[pltpu.SemaphoreType.DMA((plane, rows))],
    )(*blocks)


def correlate_kernel(sizes, count, *refs):
    me = position()
    cols, rows, groups, inputs = sizes
    sources = cols * rows * groups
    out, scratch, sem = refs[-2], refs[-3], refs[-1]
    apart = refs[0].shape[0] == rows
    got, outs = (refs[: cols * groups], refs[cols * groups : -3]) if apart else (refs[0], refs[1:-3])
    width = scratch.shape[0] // 2 * 128
    spec_count = width // inputs
    tiles = width // 128
    for part in range(2):
        for tile in range(tiles):
            lanes = slice(tile * 128, (tile + 1) * 128)
            if not apart:
                scratch[part * tiles + tile] = got[:, part, :, lanes].astype(jnp.float32).reshape(sources * count, 128)
                continue
            for q, block in enumerate(got):
                origin = lax.rem(me[2] + (cols * groups - q), cols * groups)
                col, group = origin // groups, lax.rem(origin, groups)
                for row in range(rows):
                    at = pl.multiple_of(((col * rows + row) * groups + group) * count, 8)
                    scratch[part * tiles + tile, pl.ds(at, count), :] = block[row, part, :, lanes].astype(jnp.float32)

    def one_channel(k, carry):
        loaded = [scratch[x, pl.ds(k, sources, stride=count), :].astype(jnp.bfloat16) for x in range(2 * tiles)]
        each = tiles // inputs
        parts = [jnp.concatenate(loaded[x * each : (x + 1) * each], axis=1) for x in range(2 * inputs)]
        real, imag = parts[:inputs], parts[inputs:]
        left = jnp.concatenate([jnp.concatenate(x, axis=0) for x in (real, imag)], axis=1)
        near, far = [], []
        for col in range(cols):
            at = slice(col * rows * groups, (col + 1) * rows * groups)
            near += [x[at] for x in real] + [-x[at] for x in imag]
            far += [x[at] for x in imag] + [x[at] for x in real]
        right = jnp.concatenate([jnp.concatenate(near, axis=0), jnp.concatenate(far, axis=0)], axis=1)
        value = lax.dot_general(left, right, ROWS_ALIKE, preferred_element_type=jnp.float32) * (1.0 / spec_count)
        lanes = value.shape[1] // cols
        for row in range(rows):
            picked = jnp.concatenate(
                [value[(x * rows + row) * groups : (x * rows + row + 1) * groups] for x in range(inputs * cols)], axis=0
            ).astype(jnp.bfloat16)
            for col in range(cols):
                out[col * rows + row, k] = picked[:, col * lanes : (col + 1) * lanes]
        return carry

    lax.fori_loop(0, count, one_channel, 0, unroll=2)
    owners = cols * rows
    if len(outs) == 1:
        copies = [pltpu.make_async_copy(out, outs[0], sem.at[0])]
    else:
        copies = [pltpu.make_async_copy(out.at[lax.rem(me[0] + k, owners)], outs[k], sem.at[k]) for k in range(owners)]
    for copy in copies:
        copy.start()
    for copy in copies:
        copy.wait()


def correlate(got, sizes, apart):
    cols, rows, groups, inputs = sizes
    sources = cols * rows * groups
    count, width = got[0].shape[-2:]
    block = groups * inputs
    shape = (cols * rows, count, cols * block, 2 * rows * block)
    return pl.pallas_call(
        functools.partial(correlate_kernel, sizes, count),
        in_specs=[WHOLE] * len(got),
        out_specs=[pl.BlockSpec(memory_space=pl.ANY)] * (shape[0] if apart else 1),
        out_shape=[jax.ShapeDtypeStruct(shape[1:] if apart else shape, jnp.bfloat16)] * (shape[0] if apart else 1),
        scratch_shapes=[
            pltpu.VMEM((2 * width // 128, sources * count, 128), jnp.float32),
            pltpu.VMEM(shape, jnp.bfloat16),
            pltpu.SemaphoreType.DMA((shape[0],)),
        ],
        cost_estimate=pl.CostEstimate(
            flops=8 * count * sources * inputs * sources * width,
            bytes_accessed=4 * sources * count * width + 2 * math.prod(shape),
            transcendentals=0,
        ),
    )(*got)


def finish_kernel(sizes, first, *refs):
    me = position()
    pieces, (same, out, scratch, held, sem) = refs[:-5], refs[-5:]
    cols, rows, groups, inputs = sizes
    owners, _, width, lanes = first.shape
    total = first.shape[1] + pieces[0].shape[0]
    tiles = lanes // 128
    pitch = scratch.shape[1] // (owners * total)
    whole = [(k, first.at[k], 0) for k in range(owners)]
    whole += [(lax.rem(me[0] + (owners - k), owners), piece, 1) for k, piece in enumerate(pieces)]
    slots_of = [sum((places(kind, total) for kind in kinds), []) for kinds in CHUNKS]
    for owner, got, chunk in whole:
        for slot, place in enumerate(slots_of[chunk]):
            for tile in range(tiles):
                value = got[slot, :, tile * 128 : (tile + 1) * 128].astype(jnp.float32)
                at = pl.multiple_of((owner * total + place) * pitch, 8)
                scratch[tile, pl.ds(at, width), :] = value

    flat = held.reshape(held.shape[0], held.shape[1] * held.shape[2], 128)

    copies = []
    for half in range(held.shape[0]):

        def one_row(x, carry):
            i, rest = x // (cols * groups), x % (cols * groups)
            at = rest * inputs + i
            for tile in range(tiles):
                rows_of = pl.ds(half * 128 * pitch + x, 128, stride=pitch)
                block = scratch[tile, rows_of, :].astype(jnp.bfloat16)
                value = lax.dot_general(same[...], block, ROWS_ALIKE, preferred_element_type=jnp.float32)
                for y in range(128 // (rows * groups)):
                    part, j = divmod(tile * (128 // (rows * groups)) + y, inputs)
                    start = part * rows * groups * held.shape[2] + j * width + at
                    piece = value[y * rows * groups : (y + 1) * rows * groups]
                    flat[half, pl.ds(start, rows * groups, stride=held.shape[2]), :] = piece
            return carry

        lax.fori_loop(0, width, one_row, 0, unroll=32)
        copies.append(
            pltpu.make_async_copy(
                held.at[half, :, pl.ds(0, out.shape[1])], out.at[:, :, pl.ds(half * 128, 128)], sem.at[half]
            )
        )
        copies[-1].start()
    for copy in copies:
        copy.wait()


def finish(first, pieces, sizes):
    cols, rows, groups, inputs = sizes
    owners, _, width, lanes = first.shape
    total = first.shape[1] + pieces[0].shape[0]
    channels = owners * total
    if channels % 128 or 128 % (rows * groups):
        order = np.argsort(sum((places(kind, total) for kinds in CHUNKS for kind in kinds), []))
        second = jnp.stack(pieces)[(position()[0] - jnp.arange(owners)) % owners]
        value = jnp.concatenate([first, second], axis=1)[:, order]
        value = value.reshape(channels, inputs, cols, groups, 2, inputs, rows, groups)
        return value.transpose(4, 6, 7, 5, 2, 3, 1, 0).reshape(lanes * width, channels).astype(jnp.float32)
    return pl.pallas_call(
        functools.partial(finish_kernel, sizes),
        in_specs=[WHOLE] * (owners + 2),
        out_specs=pl.BlockSpec(memory_space=pl.ANY),
        out_shape=jax.ShapeDtypeStruct((2 * rows * groups, inputs * width, channels), jnp.float32),
        scratch_shapes=[
            pltpu.VMEM((lanes // 128, channels * (width + PAD), 128), jnp.float32),
            pltpu.VMEM((channels // 128, 2 * rows * groups, inputs * width + PAD, 128), jnp.float32),
            pltpu.SemaphoreType.DMA((channels // 128,)),
        ],
    )(first, *pieces, jnp.eye(128, dtype=jnp.bfloat16))


def shards(voltages, tap_table):
    groups, rows, cols = (lax.axis_size(name) for name in ("freq", "row", "col"))
    inputs = voltages.shape[0]
    sizes = (cols, rows, groups, inputs)
    volts = voltages.transpose(1, 0, 2)
    owners = rows * cols
    plane = cols * groups

    blocks = list(dft(volts, tap_table, CHUNKS[0], groups, owners, rows))
    for k in range(1, rows):
        blocks[k] = lax.ppermute(blocks[k], "row", [(x, (x + k) % rows) for x in range(rows)])
    sent = dft(volts, tap_table, CHUNKS[1], groups, owners, 0)[0]
    sent = sent.reshape((-1,) + sent.shape[2:])
    second = lax.all_to_all(sent, EVERYONE, split_axis=0, concat_axis=0, tiled=True)
    blocks = list(turn([x.reshape((plane,) + x.shape[2:]) for x in blocks]))
    meshed = lambda place: place % groups * cols + place // groups
    for q in range(1, plane):
        pairs = [(meshed(x), meshed((x + q) % plane)) for x in range(plane)]
        blocks[q] = lax.ppermute(blocks[q], ("freq", "col"), pairs)
    if blocks[0].shape[2] % 8:
        stacked = jnp.stack(blocks)[(position()[2] - jnp.arange(plane)) % plane]
        stacked = stacked.reshape((cols, groups) + stacked.shape[1:]).swapaxes(1, 2)
        blocks = [stacked.reshape((-1,) + stacked.shape[3:])]

    first = correlate(blocks, sizes, False)[0]
    first = lax.all_to_all(first, OWNERS, split_axis=0, concat_axis=0, tiled=True)
    pieces = list(correlate([second], sizes, True))
    meshed = lambda owner: owner % rows * cols + owner // rows
    for k in range(1, owners):
        pairs = [(meshed(x), meshed((x + k) % owners)) for x in range(owners)]
        pieces[k] = lax.ppermute(pieces[k], OWNERS[::-1], pairs)
    result = finish(first, pieces, sizes)
    block = groups * inputs
    return result.reshape(2, rows, block, cols * block, -1).transpose(4, 0, 1, 2, 3)


def solution(mesh):
    in_specs = (P(("row", "col", "freq"), None, None), P())
    out_specs = P("freq", None, None, "col", "row")
    return jax.shard_map(shards, mesh=mesh, in_specs=in_specs, out_specs=out_specs, check_vma=False)
```
